512 devices in a mesh: dp: 32 (over z, x), seq: 16 (over y, core).
Axes of the slice: x: 4, y: 8, z: 8, core: 2. Of those that a mesh axis runs over, the one named last changes fastest.
Arguments:
- tokens: bfloat16 [32, 8192, 2048], P('dp', 'seq'), may hold values from -60 to 60
- in_gain: float32 [2048], replicated, may hold values from 0.1 to 1.9
- in_weight: bfloat16 [2048, 2304], P('dp'), may hold values from -0.125 to 0.125
- conv_weight: float32 [4, 2304], replicated, may hold values from -5 to 5
- conv_bias: float32 [2304], replicated, may hold values from -3 to 3
- log_decay: float32 [32, 32, 8192], P('dp', None, 'seq'), may hold values from -0.9 to 0
- skip: float32 [32], replicated, may hold values from 0.05 to 1
- out_gain: float32 [2048], replicated, may hold values from 0.1 to 1.9
- scan_order: int32 [512], replicated, may hold values from 0 to 511, each once
Outputs:
- regrouped: bfloat16 [32, 8192, 2048], P('dp', 'seq')
The draws below stay inside these ranges and needn't reach their ends.
Inputs may be any that keep to these rules, and one draw needn't show every extreme that they name: Each of the 512 positions appears once; the q-th position of a frame in the next layer's scan is scan_order[q].
All inputs are finite; a program needn't handle non-finite values.
Results may differ from the reference program's by a relative error of at most 0.008.
Values may be sent and summed in bfloat16 or wider, within the bound.
No kernel may reach another device: no remote copies, remote signals or barrier semaphores. Data moves between devices by JAX's collectives and lax.ppermute only.
A program may use at most 128 MiB of HBM per device.

```python
import math
import jax
import jax.numpy as jnp
from jax import lax

D = 2048
HALF_HEADS = 32
HEADDIM = 64
STATE = 128
KERNEL = 4
GROUP = 128
POSITIONS = 512
DIN = 2048
XBC = 2304
FRAMES = 16
VIDEO_LENGTH = 8192
VIDEO_COUNT = 32


def draw_tokens(key, part):
    random_keys = jax.random.split(jax.random.fold_in(key, 11), 3)
    base = jax.random.normal(random_keys[0], (VIDEO_COUNT, VIDEO_LENGTH, D), jnp.float32)
    column_scale = jnp.exp(jax.random.uniform(random_keys[1], (D,), jnp.float32, 0.0, math.log(10.0))) / 3.0
    row_scale = jnp.exp(jax.random.uniform(random_keys[2], (VIDEO_COUNT, VIDEO_LENGTH, 1), jnp.float32, 0.0, math.log(10.0))) / 3.0
    values = base * row_scale * column_scale
    return jnp.clip(values, -60.0, 60.0).astype(jnp.bfloat16)


def draw_conv_weight(key, part):
    random_keys = jax.random.split(jax.random.fold_in(key, 23), 2)
    channel_scale = 0.5 * jnp.exp(jax.random.uniform(random_keys[1], (1, XBC), jnp.float32, math.log(0.3), math.log(3.0)))
    base = jax.random.normal(random_keys[0], (KERNEL, XBC), jnp.float32)
    return jnp.clip(base * channel_scale, -5.0, 5.0)


def draw_log_decay(key, part):
    random_keys = jax.random.split(jax.random.fold_in(key, 37), 7)
    share = 0.5
    slow_heads = jax.random.uniform(random_keys[0], (VIDEO_COUNT, HALF_HEADS, 1), jnp.float32) < share
    slow_rate = math.log(10.0) * jax.random.uniform(random_keys[1], (VIDEO_COUNT, HALF_HEADS, 1), jnp.float32, 0.1, 0.3) / VIDEO_LENGTH
    fast_rate = jnp.exp(jax.random.uniform(random_keys[2], (VIDEO_COUNT, HALF_HEADS, 1), jnp.float32, math.log(1.0 / 50.0), math.log(1.0 / 30.0)))
    base_rate = jnp.where(slow_heads, slow_rate, fast_rate)
    frame_count = VIDEO_LENGTH // POSITIONS
    frame_factor = jnp.exp(jax.random.uniform(random_keys[3], (VIDEO_COUNT, HALF_HEADS, frame_count, 1), jnp.float32, math.log(0.5), math.log(2.0)))
    frame_factor = jnp.broadcast_to(frame_factor, (VIDEO_COUNT, HALF_HEADS, frame_count, POSITIONS)).reshape(VIDEO_COUNT, HALF_HEADS, VIDEO_LENGTH)
    token_factor = jnp.exp(jax.random.uniform(random_keys[4], (VIDEO_COUNT, HALF_HEADS, VIDEO_LENGTH), jnp.float32, math.log(0.5), math.log(2.0)))
    decay_rate = base_rate * frame_factor * token_factor
    spike_positions = jax.random.randint(random_keys[5], (VIDEO_COUNT, 2), 0, VIDEO_LENGTH)
    spike_reached = jnp.any(jnp.arange(VIDEO_LENGTH)[None, None, :] == spike_positions[:, :, None], axis=1)
    spike_penalty = jax.random.uniform(random_keys[6], (VIDEO_COUNT, HALF_HEADS, VIDEO_LENGTH), jnp.float32, 0.2, 0.5)
    return -decay_rate + jnp.where(spike_reached[:, None, :], jnp.log1p(-spike_penalty), 0.0)


def level_of(stream_key, dims, shards, low, high):
    def one(position, blocks):
        draws = jax.random.uniform(jax.random.fold_in(jax.random.fold_in(stream_key, 6), position), (blocks,), jnp.float32, low / len(shards), high / len(shards))
        return jnp.repeat(jnp.exp(draws), dims[position] // blocks).reshape((-1,) + (1,) * (len(dims) - position - 1))

    level = one(*shards[0])
    for cut in shards[1:]:
        level = level * one(*cut)
    return level


def noise(rng, extent, deviation, bound, cuts=(), held_as=jnp.bfloat16):
    result = deviation * jax.random.normal(rng, extent, jnp.float32)
    if cuts:
        result = result * level_of(rng, extent, cuts, -0.22, 0.18)
    return jnp.clip(result, -bound, bound).astype(held_as)


def setup_inputs(seed: int = 0) -> dict:
    splits = jax.random.split(jax.random.key(seed), 10)
    tokens = draw_tokens(jax.random.fold_in(splits[9], 71), 0)
    in_gain = jnp.clip(1.0 + 0.18 * jax.random.normal(splits[1], (D,), jnp.float32), 0.1, 1.9)
    in_weight = noise(splits[2], (D, XBC), D ** -0.5, 0.125, ((0, 32),))
    conv_weight = draw_conv_weight(jax.random.fold_in(splits[9], 71), 0)
    conv_bias = noise(splits[4], (XBC,), 0.5, 3.0, (), jnp.float32)
    log_decay = draw_log_decay(jax.random.fold_in(splits[9], 71), 0)
    skip = jnp.clip(jnp.exp(jax.random.uniform(splits[6], (HALF_HEADS,), jnp.float32, math.log(0.05), math.log(1.0))), 0.05, 1.0)
    out_gain = jnp.clip(1.0 + 0.18 * jax.random.normal(splits[7], (DIN,), jnp.float32), 0.1, 1.9)
    scan_order = jax.random.permutation(splits[8], POSITIONS).astype(jnp.int32)
    return {"tokens": tokens, "in_gain": in_gain, "in_weight": in_weight, "conv_weight": conv_weight, "conv_bias": conv_bias, "log_decay": log_decay, "skip": skip, "out_gain": out_gain, "scan_order": scan_order}


def group_pass(x_block, b_block, c_block, decay_block, entering):
    cumulative = jnp.cumsum(decay_block, axis=1)
    step_size = -decay_block
    scores = jnp.dot(c_block, b_block.T, preferred_element_type=jnp.float32)
    log_gap = cumulative[:, :, None] - cumulative[:, None, :]
    length = decay_block.shape[1]
    causal = jnp.arange(length)[None, :] <= jnp.arange(length)[:, None]
    decay_mask = jnp.exp(jnp.where(causal[None], log_gap, -1e+30))
    weights = (scores[None] * decay_mask * step_size[:, None, :]).astype(jnp.bfloat16)
    weights = lax.optimization_barrier(weights)
    intra = jnp.einsum('hts,shp->thp', weights.astype(jnp.float32), x_block.astype(jnp.float32), precision=lax.Precision.HIGHEST)
    closing = cumulative[:, -1:]
    scaled = ((jnp.exp(closing - cumulative) * step_size).T[:, :, None] * x_block.astype(jnp.float32)).astype(jnp.bfloat16)
    scaled = lax.optimization_barrier(scaled)
    block_state = jnp.einsum('shp,sn->hpn', scaled.astype(jnp.float32), b_block.astype(jnp.float32), precision=lax.Precision.HIGHEST)
    entering_half = lax.optimization_barrier(entering.astype(jnp.bfloat16))
    inter = jnp.einsum('tn,hpn->thp', c_block.astype(jnp.float32), entering_half.astype(jnp.float32), precision=lax.Precision.HIGHEST)
    inter = inter * jnp.exp(cumulative).T[:, :, None]
    following = jnp.exp(closing[:, 0])[:, None, None] * entering + block_state
    return (intra + inter, following)

def one_video(tokens_one, decay_one, in_gain, in_weight, conv_weight, conv_bias, skip, out_gain, scan_order):
    widened = tokens_one.astype(jnp.float32)
    inverse = lax.rsqrt(lax.optimization_barrier(jnp.mean(widened * widened, axis=1, keepdims=True)) + 1e-05)
    normed = (widened * inverse * in_gain[None, :]).astype(jnp.bfloat16)
    projected = jnp.dot(normed, in_weight, preferred_element_type=jnp.float32).astype(jnp.bfloat16)
    padded = jnp.concatenate([jnp.zeros((KERNEL - 1, XBC), jnp.bfloat16), projected], axis=0)
    mixed_pre = conv_bias[None, :] + conv_weight[0][None, :] * padded[0:VIDEO_LENGTH].astype(jnp.float32)
    for offset in range(1, KERNEL):
        mixed_pre = mixed_pre + conv_weight[offset][None, :] * padded[offset:offset + VIDEO_LENGTH].astype(jnp.float32)
    mixed = jax.nn.silu(mixed_pre).astype(jnp.bfloat16)
    inner_width = HALF_HEADS * HEADDIM
    x_heads = mixed[:, :inner_width].reshape(VIDEO_LENGTH, HALF_HEADS, HEADDIM)
    b_vectors = mixed[:, inner_width:inner_width + STATE]
    c_vectors = mixed[:, inner_width + STATE:]
    block_count = VIDEO_LENGTH // GROUP

    def advance(entering, inputs):
        x_block, b_block, c_block, decay_block = inputs
        output, following = group_pass(x_block, b_block, c_block, decay_block, entering)
        return (following, output)
    inputs = (x_heads.reshape(block_count, GROUP, HALF_HEADS, HEADDIM), b_vectors.reshape(block_count, GROUP, STATE), c_vectors.reshape(block_count, GROUP, STATE), decay_one.reshape(HALF_HEADS, block_count, GROUP).transpose(1, 0, 2))
    carried, outputs = lax.scan(advance, jnp.zeros((HALF_HEADS, HEADDIM, STATE), jnp.float32), inputs)
    ssm_out = outputs.reshape(VIDEO_LENGTH, HALF_HEADS, HEADDIM) + skip[None, :, None] * x_heads.astype(jnp.float32)
    head_scale = lax.rsqrt(lax.optimization_barrier(jnp.mean(ssm_out * ssm_out, axis=2, keepdims=True)) + 1e-05)
    normalized = (ssm_out * head_scale * out_gain.reshape(HALF_HEADS, HEADDIM)[None]).astype(jnp.bfloat16)
    framed = normalized.reshape(FRAMES, POSITIONS, inner_width)
    picked = jnp.take(framed, scan_order, axis=1)
    return picked.transpose(1, 0, 2).reshape(VIDEO_LENGTH, inner_width)

def reference(tokens, in_gain, in_weight, conv_weight, conv_bias, log_decay, skip, out_gain, scan_order):

    def per_video(video_pair):
        return one_video(video_pair[0], video_pair[1], in_gain, in_weight, conv_weight, conv_bias, skip, out_gain, scan_order)
    return lax.map(per_video, (tokens, log_decay))
```

```python
import jax
import jax.numpy as jnp
from jax import lax
from jax.experimental import pallas as pl
from jax.experimental.pallas import tpu as pltpu
from jax.sharding import PartitionSpec as P

HEADDIM = 64
STATE = 128
GROUP = 128
POSITIONS = 512
ROWS = 1024
PAD = 16
BLOCKS = ROWS // GROUP
OWN = 1024
COLS = 256
CHUNKS = 1
CHUNK = OWN // CHUNKS
EPS = 1e-05

Z, X, Y = 8, 4, 8
bf16 = jnp.bfloat16
f32 = jnp.float32


def place(z, x, y, core):
    return (z * X + x) * (2 * Y) + 2 * y + core


def far_groups():
    return [
        [place(2 * k + dz, x, y, c) for k in range(Z // 2)]
        for dz in range(2)
        for x in range(X)
        for y in range(Y)
        for c in range(2)
    ]


def near_groups():
    return [
        [place(2 * zp + dz, x, 2 * yp + dy, c) for dz in range(2) for x in range(X) for dy in range(2)]
        for zp in range(Z // 2)
        for yp in range(Y // 2)
        for c in range(2)
    ]


def spread(block, groups):
    count = len(groups[0])
    return lax.all_to_all(
        jnp.broadcast_to(block[None], (count,) + block.shape),
        ("dp", "seq"), 0, 0, axis_index_groups=groups, tiled=True,
    )


def params():
    return pltpu.CompilerParams(vmem_limit_bytes=58 * 1024 * 1024)


def whole(shape):
    return pl.BlockSpec(shape, lambda *_: (0,) * len(shape))


def project_and_mix(normed, w, taps, bias, w_all, p_all):
    for k in range(4):
        w_all[512 * k : 512 * k + 512, :] = w[:, 32 * k : 32 * k + 32, :].reshape(512, COLS)
    p_all[...] = (
        jnp.dot(normed[...], w_all[...], preferred_element_type=f32).astype(bf16).astype(f32)
    )


def mixed_rows(start, taps, bias, p_all):
    rows = p_all[pl.ds(pl.multiple_of(start + 8, 8), GROUP + 8), :]
    pre = bias[...] + taps[0:1, :] * rows[5 : 5 + GROUP]
    for k in range(1, 4):
        pre = pre + taps[k : k + 1, :] * rows[5 + k : 5 + k + GROUP]
    return (pre / (1.0 + jnp.exp(-pre))).astype(bf16)


def bc_body(normed, w, taps, bias, b_out, c_out, scores, w_all, p_all):
    project_and_mix(normed, w, taps, bias, w_all, p_all)

    def one(j, carry):
        start = pl.multiple_of(j * GROUP, GROUP)
        mixed = mixed_rows(start, taps, bias, p_all)
        b, c = mixed[:, :STATE], mixed[:, STATE:]
        b_out[pl.ds(start, GROUP), :] = b
        c_out[pl.ds(start, GROUP), :] = c
        scores[pl.ds(start, GROUP), :] = lax.dot_general(
            c, b, (((1,), (1,)), ((), ())), preferred_element_type=f32
        )
        return carry

    lax.fori_loop(0, BLOCKS, one, 0)


def bc_kernel(normed, w, taps, bias):
    return pl.pallas_call(
        bc_body,
        out_shape=(
            jax.ShapeDtypeStruct((ROWS, STATE), bf16),
            jax.ShapeDtypeStruct((ROWS, STATE), bf16),
            jax.ShapeDtypeStruct((ROWS, GROUP), f32),
        ),
        grid=(1,),
        in_specs=[
            whole(normed.shape),
            pl.BlockSpec((16, 128, COLS), lambda i: (0, 0, 0)),
            whole(taps.shape),
            whole(bias.shape),
        ],
        out_specs=(whole((ROWS, STATE)), whole((ROWS, STATE)), whole((ROWS, GROUP))),
        scratch_shapes=[pltpu.VMEM((2048, COLS), bf16), pltpu.VMEM((PAD + ROWS, COLS), f32)],
        compiler_params=params(),
        name="bc",
    )(normed, w, taps, bias)


def heads_body(
    normed, w, taps, bias, b_all, c_all, scores_all, cum_r, step_r, cum_c, step_c, skip,
    local, state, w_all, p_all,
):
    project_and_mix(normed, w, taps, bias, w_all, p_all)
    state[...] = jnp.zeros_like(state)
    row = lax.broadcasted_iota(jnp.int32, (GROUP, GROUP), 0)
    lane = lax.broadcasted_iota(jnp.int32, (GROUP, GROUP), 1)
    causal = lane <= row
    first = lane < HEADDIM

    def one(j, carry):
        start = pl.multiple_of(j * GROUP, GROUP)
        here = pl.ds(start, GROUP)
        mixed = mixed_rows(start, taps, bias, p_all)
        b = b_all[here, :]
        c = c_all[here, :]
        scores = scores_all[here, :]
        for pair in range(COLS // 128):
            wide = slice(128 * pair, 128 * pair + 128)
            x = mixed[:, wide].astype(f32)
            cums, steps, weights = [], [], []
            for h in (2 * pair, 2 * pair + 1):
                cum = jnp.broadcast_to(cum_c[0, here, h : h + 1], (GROUP, GROUP))
                gap = cum - cum_r[0, h : h + 1, here]
                decay = jnp.exp(jnp.where(causal, gap, -1e30))
                weights.append((scores * decay * step_r[0, h : h + 1, here]).astype(bf16))
                cums.append(cum)
                steps.append(jnp.broadcast_to(step_c[0, here, h : h + 1], (GROUP, GROUP)))
            both = jnp.concatenate(weights, axis=1)
            apart = jnp.concatenate(
                [jnp.where(first, x, 0.0).astype(bf16), jnp.where(first, 0.0, x).astype(bf16)], axis=0
            )
            intra = jnp.dot(both, apart, preferred_element_type=f32)
            cum = jnp.where(first, cums[0], cums[1])
            step = jnp.where(first, steps[0], steps[1])
            closing = cum[GROUP - 1 : GROUP, :]
            scaled = (jnp.exp(closing - cum) * step * x).astype(bf16)
            block_state = lax.dot_general(
                b, scaled, (((0,), (0,)), ((), ())), preferred_element_type=f32
            )
            entering = state[pair]
            inter = jnp.exp(cum) * jnp.dot(c, entering.astype(bf16), preferred_element_type=f32)
            local[here, wide] = intra + inter + skip[:, wide] * x
            state[pair] = jnp.exp(closing) * entering + block_state
        return carry

    lax.fori_loop(0, BLOCKS, one, 0)


def heads_kernel(normed, w, first_step, taps, bias, b_all, c_all, scores, cum_r, step_r, cum_c, step_c, skip):
    steps = taps.shape[1] // COLS
    heads = COLS // HEADDIM
    return pl.pallas_call(
        heads_body,
        out_shape=(
            jax.ShapeDtypeStruct((ROWS, steps * COLS), f32),
            jax.ShapeDtypeStruct((steps * COLS // 128, STATE, 128), f32),
        ),
        grid=(steps,),
        in_specs=[
            whole(normed.shape),
            pl.BlockSpec((16, 128, COLS), lambda i: (0, 0, i + first_step)),
            pl.BlockSpec((4, COLS), lambda i: (0, i)),
            pl.BlockSpec((1, COLS), lambda i: (0, i)),
            whole(b_all.shape),
            whole(c_all.shape),
            whole(scores.shape),
            pl.BlockSpec((1, heads, ROWS), lambda i: (i, 0, 0)),
            pl.BlockSpec((1, heads, ROWS), lambda i: (i, 0, 0)),
            pl.BlockSpec((1, ROWS, heads), lambda i: (i, 0, 0)),
            pl.BlockSpec((1, ROWS, heads), lambda i: (i, 0, 0)),
            pl.BlockSpec((1, COLS), lambda i: (0, i)),
        ],
        out_specs=(
            pl.BlockSpec((ROWS, COLS), lambda i: (0, i)),
            pl.BlockSpec((COLS // 128, STATE, 128), lambda i: (i, 0, 0)),
        ),
        scratch_shapes=[pltpu.VMEM((2048, COLS), bf16), pltpu.VMEM((PAD + ROWS, COLS), f32)],
        compiler_params=params(),
        name="heads",
    )(normed, w, taps, bias, b_all, c_all, scores, cum_r, step_r, cum_c, step_c, skip)


def chain_body(parts, out):
    entering = jnp.zeros(out.shape[1:], f32)
    for y in range(Y):
        out[y] = entering.astype(bf16)
        fade = parts[y, STATE : STATE + 1, :].astype(f32) + parts[y, STATE + 1 : STATE + 2, :].astype(f32)
        entering = fade * entering + parts[y, :STATE, :].astype(f32)


def chain_kernel(parts):
    return pl.pallas_call(
        chain_body,
        out_shape=jax.ShapeDtypeStruct((Y, STATE, parts.shape[2]), bf16),
        compiler_params=params(),
        name="chain",
    )(parts)


def finish_body(local, c_all, entering, cum, gain, order, out):
    lane = lax.broadcasted_iota(jnp.int32, (GROUP, GROUP), 1)
    row = lax.broadcasted_iota(jnp.int32, (GROUP, GROUP), 0)
    same_head = jnp.where((lane < HEADDIM) == (row < HEADDIM), 1.0 / HEADDIM, 0.0).astype(bf16)
    position = lax.broadcasted_iota(jnp.int32, (POSITIONS, POSITIONS), 1)
    pick = jnp.where(position == order[...], 1.0, 0.0).astype(bf16)
    first = lax.broadcasted_iota(jnp.int32, (1, 128), 1) < HEADDIM
    for frame in range(ROWS // POSITIONS):
        here = slice(frame * POSITIONS, (frame + 1) * POSITIONS)
        parts = []
        for pair in range(COLS // 128):
            wide = slice(128 * pair, 128 * pair + 128)
            inter = jnp.dot(c_all[here, :], entering[pair], preferred_element_type=f32)
            fade = jnp.exp(
                jnp.where(first, cum[0, here, 2 * pair : 2 * pair + 1], cum[0, here, 2 * pair + 1 : 2 * pair + 2])
            )
            ssm = local[here, wide] + fade * inter
            square = ssm * ssm
            high = square.astype(bf16)
            low = (square - high.astype(f32)).astype(bf16)
            mean = jnp.dot(high, same_head, preferred_element_type=f32) + jnp.dot(
                low, same_head, preferred_element_type=f32
            )
            parts.append((ssm * lax.rsqrt(mean + EPS) * gain[:, wide]).astype(bf16))
        normalized = jnp.concatenate(parts, axis=1)
        picked = jnp.dot(pick, normalized, preferred_element_type=f32).astype(bf16)
        out[:, frame] = picked.reshape(2 * Y, POSITIONS // (2 * Y), COLS)


def finish_kernel(local, c_all, entering, cum, gain, order):
    steps = local.shape[1] // COLS
    heads = COLS // HEADDIM
    piece = POSITIONS // (2 * Y)
    return pl.pallas_call(
        finish_body,
        out_shape=jax.ShapeDtypeStruct((2 * Y, 2, piece, local.shape[1]), bf16),
        grid=(steps,),
        in_specs=[
            pl.BlockSpec((ROWS, COLS), lambda i: (0, i)),
            whole(c_all.shape),
            pl.BlockSpec((COLS // 128, STATE, 128), lambda i: (i, 0, 0)),
            pl.BlockSpec((1, ROWS, heads), lambda i: (i, 0, 0)),
            pl.BlockSpec((1, COLS), lambda i: (0, i)),
            whole(order.shape),
        ],
        out_specs=pl.BlockSpec((2 * Y, 2, piece, COLS), lambda i: (0, 0, 0, i)),
        compiler_params=params(),
        name="finish",
    )(local, c_all, entering, cum, gain, order)


def regroup_body(*refs):
    *parts, out = refs
    row = lax.broadcasted_iota(jnp.int32, (POSITIONS, POSITIONS), 0)
    col = lax.broadcasted_iota(jnp.int32, (POSITIONS, POSITIONS), 1)
    piece = POSITIONS // (2 * Y)
    pick = jnp.where(col == (row % (2 * Y)) * piece + row // (2 * Y), 1.0, 0.0).astype(bf16)
    for g, part in enumerate(parts):
        for c in range(2):
            rows = part[:, c].reshape(POSITIONS, CHUNK)
            picked = jnp.dot(pick, rows, preferred_element_type=f32).astype(bf16)
            out[:, c * OWN + g * CHUNK : c * OWN + (g + 1) * CHUNK] = picked


def regroup_kernel(parts):
    return pl.pallas_call(
        regroup_body,
        out_shape=jax.ShapeDtypeStruct((POSITIONS, 2 * OWN), bf16),
        compiler_params=params(),
        name="regroup",
    )(*parts)


def on_device(
    tokens, in_gain, in_weight, conv_weight, conv_bias, log_decay, skip, out_gain, scan_order
):
    seq = lax.axis_index("seq")
    core = seq % 2
    y = seq // 2
    swap = [(i, i ^ 1) for i in range(2 * Y)]
    onward = [(i, i + 2) for i in range(2 * Y - 2)]
    head_count = OWN // HEADDIM

    def own_part(a):
        return lax.dynamic_slice_in_dim(a, core * OWN, OWN, a.ndim - 1)

    weight = jnp.concatenate([in_weight[:, 2 * OWN :], own_part(in_weight)], axis=1)
    half = lax.dynamic_slice_in_dim(weight, (y % 2) * 32, 32, 0)
    far = spread(half, far_groups()).reshape(128, 2 * STATE + OWN)
    cuts = [0] + [2 * STATE + (g + 1) * CHUNK for g in range(CHUNKS)]
    chunks = [spread(far[:, a:b], near_groups()) for a, b in zip(cuts, cuts[1:])]

    own = tokens[0]
    sibling = lax.ppermute(own, "seq", swap)
    tail = jnp.where(core == 1, own[POSITIONS - PAD :], sibling[POSITIONS - PAD :])
    tail = lax.ppermute(tail, "seq", onward)
    even = jnp.where(core == 0, own, sibling)
    odd = jnp.where(core == 0, sibling, own)
    widened = jnp.concatenate([tail, even, odd], axis=0).astype(f32)
    inverse = lax.rsqrt(jnp.mean(widened * widened, axis=1, keepdims=True) + EPS)
    normed = (widened * inverse * in_gain[None, :]).astype(bf16)

    def own_heads(which):
        return lax.dynamic_slice_in_dim(log_decay[0], which * head_count, head_count, 0)

    mine = own_heads(core)
    other = lax.ppermute(own_heads(1 - core), "seq", swap)
    decay = jnp.concatenate(
        [jnp.where(core == 0, mine, other), jnp.where(core == 0, other, mine)], axis=1
    )
    blocked = decay.reshape(head_count, BLOCKS, GROUP)
    cumulative = jnp.cumsum(blocked, axis=2)
    closings = cumulative[:, :, -1]
    before = jnp.concatenate(
        [jnp.zeros((head_count, 1), f32), jnp.cumsum(closings, axis=1)], axis=1
    )
    from_start = (cumulative + before[:, :BLOCKS, None]).reshape(head_count, ROWS)
    fade = jnp.exp(before[:, BLOCKS])
    heads = COLS // HEADDIM

    def by_step(a):
        return a.reshape(head_count // heads, heads, ROWS)

    cum_r = by_step(cumulative)
    step_r = by_step(-decay)
    cum_c = cum_r.transpose(0, 2, 1)
    step_c = step_r.transpose(0, 2, 1)
    whole_c = by_step(from_start).transpose(0, 2, 1)

    own_taps, own_bias = own_part(conv_weight[:, : 2 * OWN]), own_part(conv_bias[None, : 2 * OWN])
    own_skip = jnp.repeat(
        lax.dynamic_slice_in_dim(skip, core * head_count, head_count, 0), HEADDIM
    )[None, :]
    own_gain = own_part(out_gain[None, :])
    fade_rows = jnp.repeat(fade, HEADDIM).reshape(OWN // 128, 1, 128)
    fade_high = fade_rows.astype(bf16)
    fade_low = (fade_rows - fade_high.astype(f32)).astype(bf16)
    order = scan_order[:, None]

    b_all, c_all, scores = bc_kernel(
        normed, chunks[0], conv_weight[:, 2 * OWN :], conv_bias[None, 2 * OWN :]
    )
    same_core = [list(range(c, 2 * Y, 2)) for c in range(2)]
    arrived = []
    for g in range(CHUNKS):
        wide = slice(g * CHUNK, (g + 1) * CHUNK)
        steps = slice(g * CHUNK // COLS, (g + 1) * CHUNK // COLS)
        pairs = slice(g * CHUNK // 128, (g + 1) * CHUNK // 128)
        local, state = heads_kernel(
            normed, chunks[g], 1 if g == 0 else 0, own_taps[:, wide], own_bias[:, wide],
            b_all, c_all, scores, cum_r[steps], step_r[steps], cum_c[steps], step_c[steps],
            own_skip[:, wide],
        )
        count = CHUNK // 128
        sent = jnp.concatenate(
            [
                state.astype(bf16),
                fade_high[pairs],
                fade_low[pairs],
                jnp.zeros((count, 14, 128), bf16),
            ],
            axis=1,
        )
        per = 128 * count // Y
        if per != 128:
            sent = sent.reshape(count, STATE + 16, 128 // per, per).transpose(0, 2, 1, 3)
            sent = sent.reshape(Y, STATE + 16, per)
        parts = lax.all_to_all(sent, "seq", 0, 0, axis_index_groups=same_core, tiled=True)
        entering = lax.all_to_all(
            chain_kernel(parts), "seq", 0, 0, axis_index_groups=same_core, tiled=True
        )
        if per != 128:
            entering = entering.reshape(count, 128 // per, STATE, per).transpose(0, 2, 1, 3)
            entering = entering.reshape(count, STATE, 128)
        outgoing = finish_kernel(
            local, c_all, entering, whole_c[steps], own_gain[:, wide], order
        )
        back = lax.all_to_all(outgoing, "seq", 0, 0, tiled=True)
        arrived.append(back.reshape(Y, 2, 2, POSITIONS // (2 * Y), CHUNK))
    return regroup_kernel(arrived)[None]


def solution(mesh):
    in_specs = (
        P("dp", "seq", None),
        P(),
        P("dp", None),
        P(),
        P(),
        P("dp", None, "seq"),
        P(),
        P(),
        P(),
    )
    out_specs = P("dp", "seq", None)
    return jax.shard_map(
        on_device, mesh=mesh, in_specs=in_specs, out_specs=out_specs, check_vma=False
    )
```

```python
import jax
import jax.numpy as jnp
from jax import lax
from jax.experimental import pallas as pl
from jax.experimental.pallas import tpu as pltpu
from jax.sharding import PartitionSpec as P

HEADDIM = 64
STATE = 128
GROUP = 128
POSITIONS = 512
ROWS = 1024
PAD = 16
BLOCKS = ROWS // GROUP
OWN = 1024
COLS = 256
CHUNKS = 2
CHUNK = OWN // CHUNKS
EPS = 1e-05

Z, X, Y = 8, 4, 8
bf16 = jnp.bfloat16
f32 = jnp.float32


def place(z, x, y, core):
    return (z * X + x) * (2 * Y) + 2 * y + core


def far_groups():
    return [
        [place(2 * k + dz, x, y, c) for k in range(Z // 2)]
        for dz in range(2)
        for x in range(X)
        for y in range(Y)
        for c in range(2)
    ]


def near_groups():
    return [
        [place(2 * zp + dz, x, y, c) for dz in range(2) for x in range(X)]
        for zp in range(Z // 2)
        for y in range(Y)
        for c in range(2)
    ]


def spread(block, groups):
    count = len(groups[0])
    return lax.all_to_all(
        jnp.broadcast_to(block[None], (count,) + block.shape),
        ("dp", "seq"), 0, 0, axis_index_groups=groups, tiled=True,
    )


def params():
    return pltpu.CompilerParams(vmem_limit_bytes=58 * 1024 * 1024)


def whole(shape):
    return pl.BlockSpec(shape, lambda *_: (0,) * len(shape))


def project_and_mix(normed, w, taps, bias, w_all, p_all):
    for k in range(4):
        w_all[512 * k : 512 * k + 512, :] = w[:, 64 * k : 64 * k + 64, :].reshape(512, COLS)
    p_all[...] = (
        jnp.dot(normed[...], w_all[...], preferred_element_type=f32).astype(bf16).astype(f32)
    )


def mixed_rows(start, taps, bias, p_all):
    rows = p_all[pl.ds(pl.multiple_of(start + 8, 8), GROUP + 8), :]
    pre = bias[...] + taps[0:1, :] * rows[5 : 5 + GROUP]
    for k in range(1, 4):
        pre = pre + taps[k : k + 1, :] * rows[5 + k : 5 + k + GROUP]
    return (pre / (1.0 + jnp.exp(-pre))).astype(bf16)


def bc_body(normed, w, taps, bias, b_out, c_out, scores, w_all, p_all):
    project_and_mix(normed, w, taps, bias, w_all, p_all)

    def one(j, carry):
        start = pl.multiple_of(j * GROUP, GROUP)
        mixed = mixed_rows(start, taps, bias, p_all)
        b, c = mixed[:, :STATE], mixed[:, STATE:]
        b_out[pl.ds(start, GROUP), :] = b
        c_out[pl.ds(start, GROUP), :] = c
        scores[pl.ds(start, GROUP), :] = lax.dot_general(
            c, b, (((1,), (1,)), ((), ())), preferred_element_type=f32
        )
        return carry

    lax.fori_loop(0, BLOCKS, one, 0)


def bc_kernel(normed, w, taps, bias):
    return pl.pallas_call(
        bc_body,
        out_shape=(
            jax.ShapeDtypeStruct((ROWS, STATE), bf16),
            jax.ShapeDtypeStruct((ROWS, STATE), bf16),
            jax.ShapeDtypeStruct((ROWS, GROUP), f32),
        ),
        grid=(1,),
        in_specs=[
            whole(normed.shape),
            pl.BlockSpec((8, 256, COLS), lambda i: (0, 0, 0)),
            whole(taps.shape),
            whole(bias.shape),
        ],
        out_specs=(whole((ROWS, STATE)), whole((ROWS, STATE)), whole((ROWS, GROUP))),
        scratch_shapes=[pltpu.VMEM((2048, COLS), bf16), pltpu.VMEM((PAD + ROWS, COLS), f32)],
        compiler_params=params(),
        name="bc",
    )(normed, w, taps, bias)


def heads_body(
    normed, w, taps, bias, b_all, c_all, scores_all, cum_r, step_r, cum_c, step_c, skip, fades,
    local, sent, w_all, p_all, state,
):
    project_and_mix(normed, w, taps, bias, w_all, p_all)
    state[...] = jnp.zeros_like(state)
    row = lax.broadcasted_iota(jnp.int32, (GROUP, GROUP), 0)
    lane = lax.broadcasted_iota(jnp.int32, (GROUP, GROUP), 1)
    causal = lane <= row
    first = lane < HEADDIM

    def one(j, carry):
        start = pl.multiple_of(j * GROUP, GROUP)
        here = pl.ds(start, GROUP)
        mixed = mixed_rows(start, taps, bias, p_all)
        b = b_all[here, :]
        c = c_all[here, :]
        scores = scores_all[here, :]
        for pair in range(COLS // 128):
            wide = slice(128 * pair, 128 * pair + 128)
            x = mixed[:, wide].astype(f32)
            cums, steps, weights = [], [], []
            for h in (2 * pair, 2 * pair + 1):
                cum = jnp.broadcast_to(cum_c[0, here, h : h + 1], (GROUP, GROUP))
                gap = cum - cum_r[0, h : h + 1, here]
                decay = jnp.exp(jnp.where(causal, gap, -1e30))
                weights.append((scores * decay * step_r[0, h : h + 1, here]).astype(bf16))
                cums.append(cum)
                steps.append(jnp.broadcast_to(step_c[0, here, h : h + 1], (GROUP, GROUP)))
            both = jnp.concatenate(weights, axis=1)
            apart = jnp.concatenate(
                [jnp.where(first, x, 0.0).astype(bf16), jnp.where(first, 0.0, x).astype(bf16)], axis=0
            )
            intra = jnp.dot(both, apart, preferred_element_type=f32)
            cum = jnp.where(first, cums[0], cums[1])
            step = jnp.where(first, steps[0], steps[1])
            closing = cum[GROUP - 1 : GROUP, :]
            scaled = (jnp.exp(closing - cum) * step * x).astype(bf16)
            block_state = lax.dot_general(
                b, scaled, (((0,), (0,)), ((), ())), preferred_element_type=f32
            )
            entering = state[pair]
            inter = jnp.exp(cum) * jnp.dot(c, entering.astype(bf16), preferred_element_type=f32)
            local[here, wide] = intra + inter + skip[:, wide] * x
            state[pair] = jnp.exp(closing) * entering + block_state
        return carry

    lax.fori_loop(0, BLOCKS, one, 0)
    pairs = COLS // 128
    slab = STATE // Y
    fade_row = sent.shape[1] - PAD
    for y in range(Y):
        for pair in range(pairs):
            at = pl.multiple_of((pl.program_id(0) * pairs + pair) * slab, slab)
            sent[y, pl.ds(at, slab), :] = state[pair, slab * y : slab * y + slab, :].astype(bf16)
        sent[y, fade_row:, :] = fades[...]


def heads_kernel(
    normed, w, first_step, taps, bias, b_all, c_all, scores, cum_r, step_r, cum_c, step_c, skip, fades
):
    steps = taps.shape[1] // COLS
    heads = COLS // HEADDIM
    return pl.pallas_call(
        heads_body,
        out_shape=(
            jax.ShapeDtypeStruct((ROWS, steps * COLS), f32),
            jax.ShapeDtypeStruct((Y, steps * COLS // 128 * (STATE // Y) + PAD, 128), bf16),
        ),
        grid=(steps,),
        in_specs=[
            whole(normed.shape),
            pl.BlockSpec((8, 256, COLS), lambda i: (0, 0, i + first_step)),
            pl.BlockSpec((4, COLS), lambda i: (0, i)),
            pl.BlockSpec((1, COLS), lambda i: (0, i)),
            whole(b_all.shape),
            whole(c_all.shape),
            whole(scores.shape),
            pl.BlockSpec((1, heads, ROWS), lambda i: (i, 0, 0)),
            pl.BlockSpec((1, heads, ROWS), lambda i: (i, 0, 0)),
            pl.BlockSpec((1, ROWS, heads), lambda i: (i, 0, 0)),
            pl.BlockSpec((1, ROWS, heads), lambda i: (i, 0, 0)),
            pl.BlockSpec((1, COLS), lambda i: (0, i)),
            whole(fades.shape),
        ],
        out_specs=(
            pl.BlockSpec((ROWS, COLS), lambda i: (0, i)),
            whole((Y, steps * COLS // 128 * (STATE // Y) + PAD, 128)),
        ),
        scratch_shapes=[
            pltpu.VMEM((2048, COLS), bf16),
            pltpu.VMEM((PAD + ROWS, COLS), f32),
            pltpu.VMEM((COLS // 128, STATE, 128), f32),
        ],
        compiler_params=params(),
        name="heads",
    )(normed, w, taps, bias, b_all, c_all, scores, cum_r, step_r, cum_c, step_c, skip, fades)


def chain_body(parts, out):
    slab = STATE // Y
    pairs = CHUNK // 128
    for g in range(CHUNKS):
        base = g * (pairs * slab + PAD)
        for pair in range(pairs):
            rows = slice(base + pair * slab, base + pair * slab + slab)
            to = slice((g * pairs + pair) * slab, (g * pairs + pair + 1) * slab)
            entering = jnp.zeros((slab, 128), f32)
            for y in range(Y):
                out[y, to, :] = entering.astype(bf16)
                fades = parts[y, base + pairs * slab : base + pairs * slab + PAD, :].astype(f32)
                fade = fades[pair : pair + 1] + fades[pairs + pair : pairs + pair + 1]
                entering = fade * entering + parts[y, rows, :].astype(f32)


def chain_kernel(parts):
    return pl.pallas_call(
        chain_body,
        out_shape=jax.ShapeDtypeStruct((Y, parts.shape[1] - CHUNKS * PAD, 128), bf16),
        compiler_params=params(),
        name="chain",
    )(parts)


def finish_body(local, c_all, entering, cum, gain, order, out):
    lane = lax.broadcasted_iota(jnp.int32, (GROUP, GROUP), 1)
    row = lax.broadcasted_iota(jnp.int32, (GROUP, GROUP), 0)
    same_head = jnp.where((lane < HEADDIM) == (row < HEADDIM), 1.0 / HEADDIM, 0.0).astype(bf16)
    position = lax.broadcasted_iota(jnp.int32, (POSITIONS, POSITIONS), 1)
    pick = jnp.where(position == order[...], 1.0, 0.0).astype(bf16)
    first = lax.broadcasted_iota(jnp.int32, (1, 128), 1) < HEADDIM
    for frame in range(ROWS // POSITIONS):
        here = slice(frame * POSITIONS, (frame + 1) * POSITIONS)
        parts = []
        for pair in range(COLS // 128):
            wide = slice(128 * pair, 128 * pair + 128)
            state = entering[:, pair * (STATE // Y) : (pair + 1) * (STATE // Y), :].reshape(STATE, 128)
            inter = jnp.dot(c_all[here, :], state, preferred_element_type=f32)
            fade = jnp.exp(
                jnp.where(first, cum[0, here, 2 * pair : 2 * pair + 1], cum[0, here, 2 * pair + 1 : 2 * pair + 2])
            )
            ssm = local[here, wide] + fade * inter
            square = ssm * ssm
            high = square.astype(bf16)
            low = (square - high.astype(f32)).astype(bf16)
            mean = jnp.dot(high, same_head, preferred_element_type=f32) + jnp.dot(
                low, same_head, preferred_element_type=f32
            )
            parts.append((ssm * lax.rsqrt(mean + EPS) * gain[:, wide]).astype(bf16))
        normalized = jnp.concatenate(parts, axis=1)
        picked = jnp.dot(pick, normalized, preferred_element_type=f32).astype(bf16)
        out[:, frame] = picked.reshape(2 * Y, POSITIONS // (2 * Y), COLS)


def finish_kernel(local, c_all, entering, g, cum, gain, order):
    steps = local.shape[1] // COLS
    heads = COLS // HEADDIM
    piece = POSITIONS // (2 * Y)
    return pl.pallas_call(
        finish_body,
        out_shape=jax.ShapeDtypeStruct((2 * Y, 2, piece, local.shape[1]), bf16),
        grid=(steps,),
        in_specs=[
            pl.BlockSpec((ROWS, COLS), lambda i: (0, i)),
            whole(c_all.shape),
            pl.BlockSpec((Y, COLS // 128 * (STATE // Y), 128), lambda i: (0, g * steps + i, 0)),
            pl.BlockSpec((1, ROWS, heads), lambda i: (i, 0, 0)),
            pl.BlockSpec((1, COLS), lambda i: (0, i)),
            whole(order.shape),
        ],
        out_specs=pl.BlockSpec((2 * Y, 2, piece, COLS), lambda i: (0, 0, 0, i)),
        compiler_params=params(),
        name="finish",
    )(local, c_all, entering, cum, gain, order)


def regroup_body(part, *refs):
    out = refs[-1]
    row = lax.broadcasted_iota(jnp.int32, (POSITIONS, POSITIONS), 0)
    col = lax.broadcasted_iota(jnp.int32, (POSITIONS, POSITIONS), 1)
    piece = POSITIONS // (2 * Y)
    pick = jnp.where(col == (row % (2 * Y)) * piece + row // (2 * Y), 1.0, 0.0).astype(bf16)
    rows = part[...].reshape(POSITIONS, CHUNK)
    out[...] = jnp.dot(pick, rows, preferred_element_type=f32).astype(bf16)


def regroup_kernel(part, out, g):
    earlier = [] if out is None else [out]
    return pl.pallas_call(
        regroup_body,
        out_shape=jax.ShapeDtypeStruct((POSITIONS, 2 * OWN), bf16),
        grid=(2,),
        in_specs=[pl.BlockSpec((Y, None, 2, POSITIONS // (2 * Y), CHUNK), lambda c: (0, c, 0, 0, 0))]
        + [pl.BlockSpec(memory_space=pl.ANY) for _ in earlier],
        out_specs=pl.BlockSpec((POSITIONS, CHUNK), lambda c: (0, c * CHUNKS + g)),
        input_output_aliases={1: 0} if earlier else {},
        compiler_params=params(),
        name="regroup",
    )(part, *earlier)


def on_device(
    tokens, in_gain, in_weight, conv_weight, conv_bias, log_decay, skip, out_gain, scan_order
):
    seq = lax.axis_index("seq")
    core = seq % 2
    swap = [(i, i ^ 1) for i in range(2 * Y)]
    onward = [(i, i + 2) for i in range(2 * Y - 2)]
    head_count = OWN // HEADDIM

    def own_part(a):
        return lax.dynamic_slice_in_dim(a, core * OWN, OWN, a.ndim - 1)

    weight = jnp.concatenate([in_weight[:, 2 * OWN :], own_part(in_weight)], axis=1)
    far = spread(weight, far_groups()).reshape(256, 2 * STATE + OWN)
    cuts = [0] + [2 * STATE + (g + 1) * CHUNK for g in range(CHUNKS)]
    far_chunks = [far[:, a:b] for a, b in zip(cuts, cuts[1:])]
    chunks = [spread(far_chunks[0], near_groups())]

    own = tokens[0]
    sibling = lax.ppermute(own, "seq", swap)
    tail = jnp.where(core == 1, own[POSITIONS - PAD :], sibling[POSITIONS - PAD :])
    tail = lax.ppermute(tail, "seq", onward)
    even = jnp.where(core == 0, own, sibling)
    odd = jnp.where(core == 0, sibling, own)

    def norm(rows):
        widened = rows.astype(f32)
        inverse = lax.rsqrt(jnp.mean(widened * widened, axis=1, keepdims=True) + EPS)
        return (widened * inverse * in_gain[None, :]).astype(bf16)

    normed = jnp.concatenate([jnp.zeros((PAD, 2048), bf16), norm(jnp.concatenate([even, odd], axis=0))], axis=0)
    tail = norm(tail)

    def own_heads(which):
        return lax.dynamic_slice_in_dim(log_decay[0], which * head_count, head_count, 0)

    mine = own_heads(core)
    other = lax.ppermute(own_heads(1 - core), "seq", swap)
    decay = jnp.concatenate(
        [jnp.where(core == 0, mine, other), jnp.where(core == 0, other, mine)], axis=1
    )
    blocked = decay.reshape(head_count, BLOCKS, GROUP)
    cumulative = jnp.cumsum(blocked, axis=2)
    closings = cumulative[:, :, -1]
    before = jnp.concatenate(
        [jnp.zeros((head_count, 1), f32), jnp.cumsum(closings, axis=1)], axis=1
    )
    from_start = (cumulative + before[:, :BLOCKS, None]).reshape(head_count, ROWS)
    fade = jnp.exp(before[:, BLOCKS])
    heads = COLS // HEADDIM

    def by_step(a):
        return a.reshape(head_count // heads, heads, ROWS)

    cum_r = by_step(cumulative)
    step_r = by_step(-decay)
    cum_c = cum_r.transpose(0, 2, 1)
    step_c = step_r.transpose(0, 2, 1)
    whole_c = by_step(from_start).transpose(0, 2, 1)

    own_taps, own_bias = own_part(conv_weight[:, : 2 * OWN]), own_part(conv_bias[None, : 2 * OWN])
    own_skip = jnp.repeat(
        lax.dynamic_slice_in_dim(skip, core * head_count, head_count, 0), HEADDIM
    )[None, :]
    own_gain = own_part(out_gain[None, :])
    fade_rows = jnp.repeat(fade, HEADDIM).reshape(OWN // 128, 128)
    fade_high = fade_rows.astype(bf16)
    fade_low = (fade_rows - fade_high.astype(f32)).astype(bf16)
    order = scan_order[:, None]
    fade_parts = []
    for g in range(CHUNKS):
        pairs = slice(g * CHUNK // 128, (g + 1) * CHUNK // 128)
        fades = jnp.concatenate([fade_high[pairs], fade_low[pairs]], axis=0)
        fade_parts.append(jnp.pad(fades, ((0, PAD - fades.shape[0]), (0, 0))))

    (
        normed, tail, cum_r, step_r, cum_c, step_c, whole_c, own_taps, own_bias, own_skip, own_gain,
        order, fade_parts, far_chunks,
    ) = lax.optimization_barrier(
        (
            normed, tail, cum_r, step_r, cum_c, step_c, whole_c, own_taps, own_bias, own_skip,
            own_gain, order, fade_parts, far_chunks,
        )
    )
    normed = lax.dynamic_update_slice(normed, tail, (0, 0))
    chunks += [spread(a, near_groups()) for a in far_chunks[1:]]

    b_all, c_all, scores = bc_kernel(
        normed, chunks[0], conv_weight[:, 2 * OWN :], conv_bias[None, 2 * OWN :]
    )
    same_core = [list(range(c, 2 * Y, 2)) for c in range(2)]
    locals_, sents = [], []
    for g in range(CHUNKS):
        wide = slice(g * CHUNK, (g + 1) * CHUNK)
        steps = slice(g * CHUNK // COLS, (g + 1) * CHUNK // COLS)
        local, sent = heads_kernel(
            normed, chunks[g], 1 if g == 0 else 0, own_taps[:, wide], own_bias[:, wide],
            b_all, c_all, scores, cum_r[steps], step_r[steps], cum_c[steps], step_c[steps],
            own_skip[:, wide], fade_parts[g],
        )
        locals_.append(local)
        sents.append(sent)
    parts = lax.all_to_all(
        jnp.concatenate(sents, axis=1), "seq", 0, 0, axis_index_groups=same_core, tiled=True
    )
    entering = lax.all_to_all(
        chain_kernel(parts), "seq", 0, 0, axis_index_groups=same_core, tiled=True
    )
    out = None
    for g in range(CHUNKS):
        wide = slice(g * CHUNK, (g + 1) * CHUNK)
        steps = slice(g * CHUNK // COLS, (g + 1) * CHUNK // COLS)
        outgoing = finish_kernel(
            locals_[g], c_all, entering, g, whole_c[steps], own_gain[:, wide], order
        )
        back = lax.all_to_all(outgoing, "seq", 0, 0, tiled=True)
        out = regroup_kernel(back.reshape(Y, 2, 2, POSITIONS // (2 * Y), CHUNK), out, g)
    return out[None]


def solution(mesh):
    in_specs = (
        P("dp", "seq", None),
        P(),
        P("dp", None),
        P(),
        P(),
        P("dp", None, "seq"),
        P(),
        P(),
        P(),
    )
    out_specs = P("dp", "seq", None)
    return jax.shard_map(
        on_device, mesh=mesh, in_specs=in_specs, out_specs=out_specs, check_vma=False
    )
```

```python
import functools

import jax
import jax.numpy as jnp
from jax import lax
from jax.experimental import pallas as pl
from jax.experimental.pallas import tpu as pltpu
from jax.sharding import PartitionSpec as P

HEADDIM = 64
STATE = 128
GROUP = 128
POSITIONS = 512
ROWS = 1024
PAD = 16
BLOCKS = ROWS // GROUP
OWN = 1024
COLS = 256
CHUNKS = 2
CHUNK = OWN // CHUNKS
EPS = 1e-05

Z, X, Y = 8, 4, 8
bf16 = jnp.bfloat16
f32 = jnp.float32


def place(z, x, y, core):
    return (z * X + x) * (2 * Y) + 2 * y + core


def far_groups():
    return [
        [place(2 * k + dz, x, y, c) for k in range(Z // 2)]
        for dz in range(2)
        for x in range(X)
        for y in range(Y)
        for c in range(2)
    ]


def near_groups():
    return [
        [place(2 * zp + dz, x, 2 * yp + dy, c) for dz in range(2) for x in range(X) for dy in range(2)]
        for zp in range(Z // 2)
        for yp in range(Y // 2)
        for c in range(2)
    ]


def spread(block, groups):
    count = len(groups[0])
    return lax.all_to_all(
        jnp.broadcast_to(block[None], (count,) + block.shape),
        ("dp", "seq"), 0, 0, axis_index_groups=groups, tiled=True,
    )


def params():
    return pltpu.CompilerParams(vmem_limit_bytes=58 * 1024 * 1024)


def whole(shape):
    return pl.BlockSpec(shape, lambda *_: (0,) * len(shape))


def project_and_mix(normed, w, taps, bias, w_all, p_all):
    for k in range(4):
        w_all[512 * k : 512 * k + 512, :] = w[:, 32 * k : 32 * k + 32, :].reshape(512, COLS)
    p_all[...] = (
        jnp.dot(normed[...], w_all[...], preferred_element_type=f32).astype(bf16).astype(f32)
    )


def mixed_rows(start, taps, bias, p_all):
    rows = p_all[pl.ds(pl.multiple_of(start + 8, 8), GROUP + 8), :]
    pre = bias[...] + taps[0:1, :] * rows[5 : 5 + GROUP]
    for k in range(1, 4):
        pre = pre + taps[k : k + 1, :] * rows[5 + k : 5 + k + GROUP]
    return (pre / (1.0 + jnp.exp(-pre))).astype(bf16)


def bc_body(normed, w, taps, bias, b_out, c_out, scores, w_all, p_all):
    project_and_mix(normed, w, taps, bias, w_all, p_all)

    def one(j, carry):
        start = pl.multiple_of(j * GROUP, GROUP)
        mixed = mixed_rows(start, taps, bias, p_all)
        b, c = mixed[:, :STATE], mixed[:, STATE:]
        b_out[pl.ds(start, GROUP), :] = b
        c_out[pl.ds(start, GROUP), :] = c
        scores[pl.ds(start, GROUP), :] = lax.dot_general(
            c, b, (((1,), (1,)), ((), ())), preferred_element_type=f32
        )
        return carry

    lax.fori_loop(0, BLOCKS, one, 0)


def bc_kernel(normed, w, taps, bias):
    return pl.pallas_call(
        bc_body,
        out_shape=(
            jax.ShapeDtypeStruct((ROWS, STATE), bf16),
            jax.ShapeDtypeStruct((ROWS, STATE), bf16),
            jax.ShapeDtypeStruct((ROWS, GROUP), f32),
        ),
        grid=(1,),
        in_specs=[
            whole(normed.shape),
            pl.BlockSpec((16, 128, COLS), lambda i: (0, 0, 0)),
            pl.BlockSpec((4, COLS), lambda i: (0, 2 * OWN // COLS)),
            pl.BlockSpec((1, COLS), lambda i: (0, 2 * OWN // COLS)),
        ],
        out_specs=(whole((ROWS, STATE)), whole((ROWS, STATE)), whole((ROWS, GROUP))),
        scratch_shapes=[pltpu.VMEM((2048, COLS), bf16), pltpu.VMEM((PAD + ROWS, COLS), f32)],
        compiler_params=params(),
        name="bc",
    )(normed, w, taps, bias)


def heads_body(
    base, core, normed, w, taps, bias, b_all, c_all, scores_all, cum_r, step_r, cum_c, step_c, skip, fades,
    local, sent, w_all, p_all, state,
):
    project_and_mix(normed, w, taps, bias, w_all, p_all)
    state[...] = jnp.zeros_like(state)
    heads = COLS // HEADDIM
    head = core[0] * (OWN // HEADDIM) + (base + pl.program_id(0)) * heads
    row = lax.broadcasted_iota(jnp.int32, (GROUP, GROUP), 0)
    lane = lax.broadcasted_iota(jnp.int32, (GROUP, GROUP), 1)
    causal = lane <= row
    first = lane < HEADDIM

    def one(j, carry):
        start = pl.multiple_of(j * GROUP, GROUP)
        here = pl.ds(start, GROUP)
        mixed = mixed_rows(start, taps, bias, p_all)
        b = b_all[here, :]
        c = c_all[here, :]
        scores = scores_all[here, :]
        for pair in range(COLS // 128):
            wide = slice(128 * pair, 128 * pair + 128)
            x = mixed[:, wide].astype(f32)
            cums, steps, weights = [], [], []
            for h in (2 * pair, 2 * pair + 1):
                cum = jnp.broadcast_to(cum_c[0, here, h : h + 1], (GROUP, GROUP))
                gap = cum - cum_r[0, h : h + 1, here]
                decay = jnp.exp(jnp.where(causal, gap, -1e30))
                weights.append((scores * decay * step_r[0, h : h + 1, here]).astype(bf16))
                cums.append(cum)
                steps.append(jnp.broadcast_to(step_c[0, here, h : h + 1], (GROUP, GROUP)))
            both = jnp.concatenate(weights, axis=1)
            apart = jnp.concatenate(
                [jnp.where(first, x, 0.0).astype(bf16), jnp.where(first, 0.0, x).astype(bf16)], axis=0
            )
            intra = jnp.dot(both, apart, preferred_element_type=f32)
            cum = jnp.where(first, cums[0], cums[1])
            step = jnp.where(first, steps[0], steps[1])
            closing = cum[GROUP - 1 : GROUP, :]
            scaled = (jnp.exp(closing - cum) * step * x).astype(bf16)
            block_state = lax.dot_general(
                b, scaled, (((0,), (0,)), ((), ())), preferred_element_type=f32
            )
            entering = state[pair]
            inter = jnp.exp(cum) * jnp.dot(c, entering.astype(bf16), preferred_element_type=f32)
            gains = jnp.where(first, skip[head + 2 * pair], skip[head + 2 * pair + 1])
            local[here, wide] = intra + inter + gains * x
            state[pair] = jnp.exp(closing) * entering + block_state
        return carry

    lax.fori_loop(0, BLOCKS, one, 0)
    pairs = COLS // 128
    slab = STATE // Y
    fade_row = sent.shape[1] - PAD
    for y in range(Y):
        for pair in range(pairs):
            at = pl.multiple_of((pl.program_id(0) * pairs + pair) * slab, slab)
            sent[y, pl.ds(at, slab), :] = state[pair, slab * y : slab * y + slab, :].astype(bf16)
        sent[y, fade_row:, :] = fades[...]


def heads_kernel(
    core, g, normed, w, first_step, taps, bias, b_all, c_all, scores, cum_r, step_r, cum_c, step_c, skip, fades
):
    steps = CHUNK // COLS
    heads = COLS // HEADDIM
    base = g * steps
    sent = (Y, CHUNK // 128 * (STATE // Y) + PAD, 128)

    def channels(i, core):
        return (0, core[0] * (OWN // COLS) + base + i)

    def step(i, core):
        return (base + i, 0, 0)

    return pl.pallas_call(
        functools.partial(heads_body, base),
        out_shape=(
            jax.ShapeDtypeStruct((ROWS, CHUNK), f32),
            jax.ShapeDtypeStruct(sent, bf16),
        ),
        grid_spec=pltpu.PrefetchScalarGridSpec(
            num_scalar_prefetch=1,
            grid=(steps,),
            in_specs=[
                whole(normed.shape),
                pl.BlockSpec((16, 128, COLS), lambda i, core: (0, 0, i + first_step)),
                pl.BlockSpec((4, COLS), channels),
                pl.BlockSpec((1, COLS), channels),
                whole(b_all.shape),
                whole(c_all.shape),
                whole(scores.shape),
                pl.BlockSpec((1, heads, ROWS), step),
                pl.BlockSpec((1, heads, ROWS), step),
                pl.BlockSpec((1, ROWS, heads), step),
                pl.BlockSpec((1, ROWS, heads), step),
                pl.BlockSpec(memory_space=pltpu.SMEM),
                pl.BlockSpec((None, PAD, 128), lambda i, core: (g, 0, 0)),
            ],
            out_specs=(
                pl.BlockSpec((ROWS, COLS), lambda i, core: (0, i)),
                whole(sent),
            ),
            scratch_shapes=[
                pltpu.VMEM((2048, COLS), bf16),
                pltpu.VMEM((PAD + ROWS, COLS), f32),
                pltpu.VMEM((COLS // 128, STATE, 128), f32),
            ],
        ),
        compiler_params=params(),
        name="heads",
    )(core, normed, w, taps, bias, b_all, c_all, scores, cum_r, step_r, cum_c, step_c, skip, fades)


def chain_body(parts, out):
    slab = STATE // Y
    pairs = CHUNK // 128
    for g in range(CHUNKS):
        base = g * (pairs * slab + PAD)
        for pair in range(pairs):
            rows = slice(base + pair * slab, base + pair * slab + slab)
            to = slice((g * pairs + pair) * slab, (g * pairs + pair + 1) * slab)
            entering = jnp.zeros((slab, 128), f32)
            for y in range(Y):
                out[y, to, :] = entering.astype(bf16)
                fades = parts[y, base + pairs * slab : base + pairs * slab + PAD, :].astype(f32)
                fade = fades[pair : pair + 1] + fades[pairs + pair : pairs + pair + 1]
                entering = fade * entering + parts[y, rows, :].astype(f32)


def chain_kernel(parts):
    return pl.pallas_call(
        chain_body,
        out_shape=jax.ShapeDtypeStruct((Y, parts.shape[1] - CHUNKS * PAD, 128), bf16),
        compiler_params=params(),
        name="chain",
    )(parts)


def finish_body(core, *refs):
    *locals_, c_all, entering, cum, gain, order, out = refs
    lane = lax.broadcasted_iota(jnp.int32, (GROUP, GROUP), 1)
    row = lax.broadcasted_iota(jnp.int32, (GROUP, GROUP), 0)
    same_head = jnp.where((lane < HEADDIM) == (row < HEADDIM), 1.0 / HEADDIM, 0.0).astype(bf16)
    position = lax.broadcasted_iota(jnp.int32, (POSITIONS, POSITIONS), 1)
    pick = jnp.where(position == order[...], 1.0, 0.0).astype(bf16)
    first = lax.broadcasted_iota(jnp.int32, (1, 128), 1) < HEADDIM
    for frame in range(ROWS // POSITIONS):
        here = slice(frame * POSITIONS, (frame + 1) * POSITIONS)
        parts = []
        step = pl.program_id(0)
        per = CHUNK // COLS
        for pair in range(COLS // 128):
            wide = slice(128 * pair, 128 * pair + 128)
            state = entering[:, pair * (STATE // Y) : (pair + 1) * (STATE // Y), :].reshape(STATE, 128)
            inter = jnp.dot(c_all[here, :], state, preferred_element_type=f32)
            fade = jnp.exp(
                jnp.where(first, cum[0, here, 2 * pair : 2 * pair + 1], cum[0, here, 2 * pair + 1 : 2 * pair + 2])
            )
            local = locals_[0][here, wide]
            for g in range(1, CHUNKS):
                local = jnp.where(step >= g * per, locals_[g][here, wide], local)
            ssm = local + fade * inter
            square = ssm * ssm
            high = square.astype(bf16)
            low = (square - high.astype(f32)).astype(bf16)
            mean = jnp.dot(high, same_head, preferred_element_type=f32) + jnp.dot(
                low, same_head, preferred_element_type=f32
            )
            parts.append((ssm * lax.rsqrt(mean + EPS) * gain[:, wide]).astype(bf16))
        normalized = jnp.concatenate(parts, axis=1)
        picked = jnp.dot(pick, normalized, preferred_element_type=f32).astype(bf16)
        out[:, frame] = picked.reshape(2 * Y, POSITIONS // (2 * Y), COLS)


def finish_kernel(core, locals_, c_all, entering, cum, gain, order):
    steps = OWN // COLS
    per = CHUNK // COLS
    heads = COLS // HEADDIM
    piece = POSITIONS // (2 * Y)

    def chunk_block(g):
        return lambda i, core: (0, jnp.clip(i - g * per, 0, per - 1))

    return pl.pallas_call(
        finish_body,
        out_shape=jax.ShapeDtypeStruct((2 * Y, 2, piece, OWN), bf16),
        grid_spec=pltpu.PrefetchScalarGridSpec(
            num_scalar_prefetch=1,
            grid=(steps,),
            in_specs=[pl.BlockSpec((ROWS, COLS), chunk_block(g)) for g in range(CHUNKS)]
            + [
                whole(c_all.shape),
                pl.BlockSpec((Y, COLS // 128 * (STATE // Y), 128), lambda i, core: (0, i, 0)),
                pl.BlockSpec((1, ROWS, heads), lambda i, core: (i, 0, 0)),
                pl.BlockSpec((1, COLS), lambda i, core: (0, core[0] * steps + i)),
                whole(order.shape),
            ],
            out_specs=pl.BlockSpec((2 * Y, 2, piece, COLS), lambda i, core: (0, 0, 0, i)),
        ),
        compiler_params=params(),
        name="finish",
    )(core, *locals_, c_all, entering, cum, gain, order)


def regroup_body(part, out):
    row = lax.broadcasted_iota(jnp.int32, (POSITIONS, POSITIONS), 0)
    col = lax.broadcasted_iota(jnp.int32, (POSITIONS, POSITIONS), 1)
    piece = POSITIONS // (2 * Y)
    pick = jnp.where(col == (row % (2 * Y)) * piece + row // (2 * Y), 1.0, 0.0).astype(bf16)
    rows = part[...].reshape(POSITIONS, OWN // 2)
    out[...] = jnp.dot(pick, rows, preferred_element_type=f32).astype(bf16)


def regroup_kernel(part):
    half = OWN // 2
    return pl.pallas_call(
        regroup_body,
        out_shape=jax.ShapeDtypeStruct((POSITIONS, 2 * OWN), bf16),
        grid=(4,),
        in_specs=[
            pl.BlockSpec(
                (Y, None, 2, POSITIONS // (2 * Y), half), lambda i: (0, i // 2, 0, 0, i % 2)
            )
        ],
        out_specs=pl.BlockSpec((POSITIONS, half), lambda i: (0, i)),
        compiler_params=params(),
        name="regroup",
    )(part)


def norm_rows(rows, gain):
    widened = rows.astype(f32)
    inverse = lax.rsqrt(jnp.mean(widened * widened, axis=1, keepdims=True) + EPS)
    return (widened * inverse * gain).astype(bf16)


def norm_body(core, own, sibling, gain, out):
    size = 64

    def one(i, carry):
        at = pl.multiple_of(i * size, size)
        mine = pl.multiple_of(PAD + core[0] * POSITIONS + at, PAD)
        other = pl.multiple_of(PAD + (1 - core[0]) * POSITIONS + at, PAD)
        out[pl.ds(mine, size), :] = norm_rows(own[pl.ds(at, size), :], gain[...])
        out[pl.ds(other, size), :] = norm_rows(sibling[pl.ds(at, size), :], gain[...])
        return carry

    out[:PAD, :] = jnp.zeros((PAD, out.shape[1]), bf16)
    lax.fori_loop(0, POSITIONS // size, one, 0)


def norm_kernel(core, own, sibling, gain):
    width = own.shape[1]
    return pl.pallas_call(
        norm_body,
        out_shape=jax.ShapeDtypeStruct((PAD + ROWS, width), bf16),
        in_specs=[pl.BlockSpec(memory_space=pltpu.SMEM)]
        + [pl.BlockSpec(memory_space=pltpu.VMEM) for _ in range(3)],
        compiler_params=params(),
        name="norm",
    )(core, own, sibling, gain)


def tail_body(rows, gain, normed, out):
    out[...] = norm_rows(rows[...], gain[...])


def tail_kernel(rows, gain, normed):
    return pl.pallas_call(
        tail_body,
        out_shape=jax.ShapeDtypeStruct(normed.shape, bf16),
        grid=(1,),
        in_specs=[whole(rows.shape), whole(gain.shape), pl.BlockSpec(memory_space=pl.ANY)],
        out_specs=pl.BlockSpec(rows.shape, lambda i: (0, 0)),
        input_output_aliases={2: 0},
        compiler_params=params(),
        name="tail",
    )(rows, gain, normed)


def decay_body(core, own, other, cum_r, step_r, cum_c, step_c, whole_c, fades):
    count = OWN // HEADDIM
    heads = COLS // HEADDIM
    mine = own[pl.ds(pl.multiple_of(core[0] * count, count), count), :]
    earlier = jnp.where(core[0] == 0, mine, other[...])
    later = jnp.where(core[0] == 0, other[...], mine)
    per = POSITIONS // GROUP
    rows = jnp.concatenate(
        [a[:, GROUP * j : GROUP * j + GROUP] for a in (earlier, later) for j in range(per)], axis=0
    )
    row = lax.broadcasted_iota(jnp.int32, (GROUP, GROUP), 0)
    lane = lax.broadcasted_iota(jnp.int32, (GROUP, GROUP), 1)
    upto = jnp.where(row <= lane, 1.0, 0.0).astype(f32)
    cum = jnp.dot(rows, upto, preferred_element_type=f32, precision=lax.Precision.HIGHEST)
    before = [jnp.zeros((count, 1), f32)]
    for j in range(BLOCKS):
        before.append(before[-1] + cum[count * j : count * j + count, GROUP - 1 : GROUP])
    since = cum + jnp.concatenate(before[:BLOCKS], axis=0)
    turned = [a.T for a in (cum, -rows, since)]
    for i in range(OWN // COLS):
        for j in range(BLOCKS):
            at = slice(GROUP * j, GROUP * j + GROUP)
            some = slice(count * j + heads * i, count * j + heads * i + heads)
            cum_r[i, :, at] = cum[some, :]
            step_r[i, :, at] = -rows[some, :]
            for out, a in zip((cum_c, step_c, whole_c), turned):
                out[i, at, :] = a[:, some]
    fade = jnp.broadcast_to(jnp.exp(before[BLOCKS]), (count, 128))
    first = lax.broadcasted_iota(jnp.int32, (1, 128), 1) < HEADDIM
    pairs = CHUNK // 128
    for g in range(CHUNKS):
        spread_out = jnp.concatenate(
            [
                jnp.where(first, fade[2 * p : 2 * p + 1], fade[2 * p + 1 : 2 * p + 2])
                for p in range(g * pairs, g * pairs + pairs)
            ],
            axis=0,
        )
        high = spread_out.astype(bf16).astype(f32)
        fill = jnp.zeros((PAD - 2 * pairs, 128), f32)
        fades[g] = jnp.concatenate([high, spread_out - high, fill], axis=0).astype(bf16)


def decay_kernel(core, own, other):
    steps = OWN // COLS
    heads = COLS // HEADDIM
    in_rows = jax.ShapeDtypeStruct((steps, heads, ROWS), f32)
    in_columns = jax.ShapeDtypeStruct((steps, ROWS, heads), f32)
    return pl.pallas_call(
        decay_body,
        out_shape=(
            in_rows, in_rows, in_columns, in_columns, in_columns,
            jax.ShapeDtypeStruct((CHUNKS, PAD, 128), bf16),
        ),
        in_specs=[pl.BlockSpec(memory_space=pltpu.SMEM)]
        + [pl.BlockSpec(memory_space=pltpu.VMEM) for _ in range(2)],
        compiler_params=params(),
        name="decay",
    )(core, own, other)


def on_device(
    tokens, in_gain, in_weight, conv_weight, conv_bias, log_decay, skip, out_gain, scan_order
):
    seq = lax.axis_index("seq")
    core = seq % 2
    y = seq // 2
    swap = [(i, i ^ 1) for i in range(2 * Y)]
    onward = [(i, i + 2) for i in range(2 * Y - 2)]
    head_count = OWN // HEADDIM
    which = core.astype(jnp.int32)[None]

    weight = jnp.concatenate(
        [in_weight[:, 2 * OWN :], lax.dynamic_slice_in_dim(in_weight, core * OWN, OWN, 1)], axis=1
    )
    half = lax.dynamic_slice_in_dim(weight, (y % 2) * 32, 32, 0)
    far = spread(half, far_groups()).reshape(128, 2 * STATE + OWN)
    cuts = [0] + [2 * STATE + (g + 1) * CHUNK for g in range(CHUNKS)]
    far_chunks = [far[:, a:b] for a, b in zip(cuts, cuts[1:])]
    chunks = [spread(far_chunks[0], near_groups())]

    own = tokens[0]
    gain = in_gain[None, :]
    sibling = lax.ppermute(own, "seq", swap)
    tail = jnp.where(core == 1, own[POSITIONS - PAD :], sibling[POSITIONS - PAD :])
    tail = lax.ppermute(tail, "seq", onward)
    normed = norm_kernel(which, own, sibling, gain)
    other = lax.dynamic_slice_in_dim(log_decay[0], (1 - core) * head_count, head_count, 0)
    decays = decay_kernel(which, log_decay[0], lax.ppermute(other, "seq", swap))
    bias = conv_bias[None, :]
    last_gain = out_gain[None, :]
    order = scan_order[:, None]

    normed, tail, decays, bias, last_gain, order, far_chunks = lax.optimization_barrier(
        (normed, tail, decays, bias, last_gain, order, far_chunks)
    )
    cum_r, step_r, cum_c, step_c, whole_c, fades = decays
    normed = tail_kernel(tail, gain, normed)
    chunks += [spread(a, near_groups()) for a in far_chunks[1:]]

    b_all, c_all, scores = bc_kernel(normed, chunks[0], conv_weight, bias)
    same_core = [list(range(c, 2 * Y, 2)) for c in range(2)]
    locals_, sents = [], []
    for g in range(CHUNKS):
        local, sent = heads_kernel(
            which, g, normed, chunks[g], 1 if g == 0 else 0, conv_weight, bias,
            b_all, c_all, scores, cum_r, step_r, cum_c, step_c, skip, fades,
        )
        locals_.append(local)
        sents.append(sent)
    parts = lax.all_to_all(
        jnp.concatenate(sents, axis=1), "seq", 0, 0, axis_index_groups=same_core, tiled=True
    )
    entering = lax.all_to_all(
        chain_kernel(parts), "seq", 0, 0, axis_index_groups=same_core, tiled=True
    )
    outgoing = finish_kernel(which, locals_, c_all, entering, whole_c, last_gain, order)
    back = lax.all_to_all(outgoing, "seq", 0, 0, tiled=True)
    return regroup_kernel(back.reshape(Y, 2, 2, POSITIONS // (2 * Y), OWN))[None]


def solution(mesh):
    in_specs = (
        P("dp", "seq", None),
        P(),
        P("dp", None),
        P(),
        P(),
        P("dp", None, "seq"),
        P(),
        P(),
        P(),
    )
    out_specs = P("dp", "seq", None)
    return jax.shard_map(
        on_device, mesh=mesh, in_specs=in_specs, out_specs=out_specs, check_vma=False
    )
```

```python
import functools

import jax
import jax.numpy as jnp
from jax import lax
from jax.experimental import pallas as pl
from jax.experimental.pallas import tpu as pltpu
from jax.sharding import PartitionSpec as P

HEADDIM = 64
STATE = 128
GROUP = 128
POSITIONS = 512
ROWS = 1024
PAD = 16
BLOCKS = ROWS // GROUP
OWN = 1024
COLS = 256
PARTS = (1, 2, 1)
LOG2E = 1.4426950408889634
EPS = 1e-05

Z, X, Y = 8, 4, 8
bf16 = jnp.bfloat16
f32 = jnp.float32


def place(z, x, y, core):
    return (z * X + x) * (2 * Y) + 2 * y + core


def far_groups():
    return [
        [place(2 * k + dz, x, y, c) for k in range(Z // 2)]
        for dz in range(2)
        for x in range(X)
        for y in range(Y)
        for c in range(2)
    ]


def near_groups():
    return [
        [place(2 * zp + dz, x, 2 * yp + dy, c) for dz in range(2) for x in range(X) for dy in range(2)]
        for zp in range(Z // 2)
        for yp in range(Y // 2)
        for c in range(2)
    ]


def spread(block, groups):
    count = len(groups[0])
    return lax.all_to_all(
        jnp.broadcast_to(block[None], (count,) + block.shape),
        ("dp", "seq"), 0, 0, axis_index_groups=groups, tiled=True,
    )


def params():
    return pltpu.CompilerParams(vmem_limit_bytes=58 * 1024 * 1024)


def whole(shape):
    return pl.BlockSpec(shape, lambda *_: (0,) * len(shape))


def project_and_mix(normed, w, taps, bias, w_all, p_all):
    for k in range(4):
        w_all[512 * k : 512 * k + 512, :] = w[:, 32 * k : 32 * k + 32, :].reshape(512, COLS)
    p_all[...] = (
        jnp.dot(normed[...], w_all[...], preferred_element_type=f32).astype(bf16).astype(f32)
    )


def mixed_rows(start, taps, bias, p_all):
    rows = p_all.at[pl.ds(pl.multiple_of(start + 8, 8), GROUP + 8), :]
    pre = bias[...] + taps[0:1, :] * rows[5 : 5 + GROUP, :]
    for k in range(1, 4):
        pre = pre + taps[k : k + 1, :] * rows[5 + k : 5 + k + GROUP, :]
    half = 0.5 * pre
    return (half + half * jnp.tanh(half)).astype(bf16)


def bc_body(normed, w, taps, bias, b_out, c_out, scores, w_all, p_all):
    project_and_mix(normed, w, taps, bias, w_all, p_all)

    def one(j, carry):
        start = pl.multiple_of(j * GROUP, GROUP)
        mixed = mixed_rows(start, taps, bias, p_all)
        b, c = mixed[:, :STATE], mixed[:, STATE:]
        b_out[pl.ds(start, GROUP), :] = b
        c_out[pl.ds(start, GROUP), :] = c
        scores[pl.ds(start, GROUP), :] = lax.dot_general(
            c, b, (((1,), (1,)), ((), ())), preferred_element_type=f32
        )
        return carry

    lax.fori_loop(0, BLOCKS, one, 0)


def bc_kernel(normed, w, taps, bias):
    return pl.pallas_call(
        bc_body,
        out_shape=(
            jax.ShapeDtypeStruct((ROWS, STATE), bf16),
            jax.ShapeDtypeStruct((ROWS, STATE), bf16),
            jax.ShapeDtypeStruct((ROWS, GROUP), f32),
        ),
        grid=(1,),
        in_specs=[
            whole(normed.shape),
            pl.BlockSpec((16, 128, COLS), lambda i: (0, 0, 0)),
            pl.BlockSpec((4, COLS), lambda i: (0, 2 * OWN // COLS)),
            pl.BlockSpec((1, COLS), lambda i: (0, 2 * OWN // COLS)),
        ],
        out_specs=(whole((ROWS, STATE)), whole((ROWS, STATE)), whole((ROWS, GROUP))),
        scratch_shapes=[pltpu.VMEM((2048, COLS), bf16), pltpu.VMEM((PAD + ROWS, COLS), f32)],
        compiler_params=params(),
        name="bc",
    )(normed, w, taps, bias)


def heads_body(
    base, core, normed, w, taps, bias, b_all, c_all, scores_all, cum_c, cum_r, e_in, e_out, skip, fades,
    *refs,
):
    local, sent, w_all, p_all, state = refs[-5:]
    i = pl.program_id(0)

    @pl.when(i == 0)
    def _():
        if base:
            sent[...] = refs[1][...]
        else:
            for y in range(Y):
                sent[y, sent.shape[1] - PAD :, :] = fades[...]

    project_and_mix(normed, w, taps, bias, w_all, p_all)
    state[...] = jnp.zeros_like(state)
    heads = COLS // HEADDIM
    pairs = COLS // 128
    head = core[0] * (OWN // HEADDIM) + (base + i) * heads
    row = lax.broadcasted_iota(jnp.int32, (GROUP, GROUP), 0)
    lane = lax.broadcasted_iota(jnp.int32, (GROUP, GROUP), 1)
    causal = lane <= row
    first = lane < HEADDIM

    def one(j, carry):
        start = pl.multiple_of(j * GROUP, GROUP)
        here = pl.ds(start, GROUP)
        mixed = mixed_rows(start, taps, bias, p_all)
        b = b_all[here, :]
        c = c_all[here, :]
        scores = scores_all[here, :]
        for pair in range(pairs):
            wide = slice(128 * pair, 128 * pair + 128)
            x = mixed[:, wide].astype(f32)
            weights = []
            for h in (2 * pair, 2 * pair + 1):
                cum = jnp.broadcast_to(cum_c[0, here, h : h + 1], (GROUP, GROUP))
                gap = cum - cum_r[0, h : h + 1, here]
                weights.append((scores * jnp.exp2(jnp.where(causal, gap, -1e30))).astype(bf16))
            both = jnp.concatenate(weights, axis=1)
            apart = jnp.concatenate(
                [jnp.where(first, x, 0.0).astype(bf16), jnp.where(first, 0.0, x).astype(bf16)], axis=0
            )
            intra = jnp.dot(both, apart, preferred_element_type=f32)
            scaled = (e_out[here, wide] * x).astype(bf16)
            block_state = lax.dot_general(
                b, scaled, (((0,), (0,)), ((), ())), preferred_element_type=f32
            )
            entering = state[pair]
            fade = e_in[here, wide]
            inter = fade * jnp.dot(c, entering.astype(bf16), preferred_element_type=f32)
            gains = jnp.where(first, skip[head + 2 * pair], skip[head + 2 * pair + 1])
            local[here, wide] = intra + inter + gains * x
            state[pair] = fade[GROUP - 1 :, :] * entering + block_state
        return carry

    lax.fori_loop(0, BLOCKS, one, 0)
    slab = STATE // Y
    for y in range(Y):
        for pair in range(pairs):
            at = pl.multiple_of(((base + i) * pairs + pair) * slab, slab)
            sent[y, pl.ds(at, slab), :] = state[pair, slab * y : slab * y + slab, :].astype(bf16)


def heads_kernel(
    core, base, steps, normed, w, first_step, taps, bias, b_all, c_all, scores, cum_c, cum_r, e_in, e_out,
    skip, fades, earlier,
):
    heads = COLS // HEADDIM
    sent = (Y, OWN // 128 * (STATE // Y) + PAD, 128)

    def channels(i, core):
        return (0, core[0] * (OWN // COLS) + base + i)

    def step(i, core):
        return (base + i, 0, 0)

    def column(i, core):
        return (0, base + i)

    return pl.pallas_call(
        functools.partial(heads_body, base),
        out_shape=(
            jax.ShapeDtypeStruct((ROWS, OWN), f32),
            jax.ShapeDtypeStruct(sent, bf16),
        ),
        grid_spec=pltpu.PrefetchScalarGridSpec(
            num_scalar_prefetch=1,
            grid=(steps,),
            in_specs=[
                whole(normed.shape),
                pl.BlockSpec((16, 128, COLS), lambda i, core: (0, 0, i + first_step)),
                pl.BlockSpec((4, COLS), channels),
                pl.BlockSpec((1, COLS), channels),
                whole(b_all.shape),
                whole(c_all.shape),
                whole(scores.shape),
                pl.BlockSpec((1, ROWS, heads), step),
                pl.BlockSpec((1, heads, ROWS), step),
                pl.BlockSpec((ROWS, COLS), column),
                pl.BlockSpec((ROWS, COLS), column),
                pl.BlockSpec(memory_space=pltpu.SMEM),
                whole(fades.shape),
            ]
            + ([pl.BlockSpec(memory_space=pl.ANY), whole(sent)] if earlier else []),
            out_specs=(
                pl.BlockSpec((ROWS, COLS), column),
                whole(sent),
            ),
            scratch_shapes=[
                pltpu.VMEM((2048, COLS), bf16),
                pltpu.VMEM((PAD + ROWS, COLS), f32),
                pltpu.VMEM((COLS // 128, STATE, 128), f32),
            ],
        ),
        input_output_aliases={14: 0, 15: 1} if earlier else {},
        compiler_params=params(),
        name="heads",
    )(
        core, normed, w, taps, bias, b_all, c_all, scores, cum_c, cum_r, e_in, e_out, skip, fades,
        *earlier,
    )


def chain_body(parts, out):
    slab = STATE // Y
    pairs = OWN // 128
    base = pairs * slab
    for pair in range(pairs):
        rows = slice(pair * slab, pair * slab + slab)
        entering = jnp.zeros((slab, 128), f32)
        for y in range(Y):
            out[y, rows, :] = entering.astype(bf16)
            fades = parts[y, base:, :].astype(f32)
            fade = fades[pair : pair + 1] + fades[pairs + pair : pairs + pair + 1]
            entering = fade * entering + parts[y, rows, :].astype(f32)


def chain_kernel(parts):
    return pl.pallas_call(
        chain_body,
        out_shape=jax.ShapeDtypeStruct((Y, parts.shape[1] - PAD, 128), bf16),
        compiler_params=params(),
        name="chain",
    )(parts)


def finish_body(core, local, c_all, entering, fade, gain, order, out):
    lane = lax.broadcasted_iota(jnp.int32, (GROUP, GROUP), 1)
    row = lax.broadcasted_iota(jnp.int32, (GROUP, GROUP), 0)
    same_head = jnp.where((lane < HEADDIM) == (row < HEADDIM), 1.0 / HEADDIM, 0.0).astype(bf16)
    position = lax.broadcasted_iota(jnp.int32, (POSITIONS, POSITIONS), 1)
    pick = jnp.where(position == order[...], 1.0, 0.0).astype(bf16)
    for frame in range(ROWS // POSITIONS):
        here = slice(frame * POSITIONS, (frame + 1) * POSITIONS)
        parts = []
        for pair in range(COLS // 128):
            wide = slice(128 * pair, 128 * pair + 128)
            state = entering[:, pair * (STATE // Y) : (pair + 1) * (STATE // Y), :].reshape(STATE, 128)
            inter = jnp.dot(c_all[here, :], state, preferred_element_type=f32)
            ssm = local[here, wide] + fade[here, wide] * inter
            square = ssm * ssm
            high = square.astype(bf16)
            low = (square - high.astype(f32)).astype(bf16)
            mean = jnp.dot(high, same_head, preferred_element_type=f32) + jnp.dot(
                low, same_head, preferred_element_type=f32
            )
            parts.append((ssm * lax.rsqrt(mean + EPS) * gain[:, wide]).astype(bf16))
        normalized = jnp.concatenate(parts, axis=1)
        picked = jnp.dot(pick, normalized, preferred_element_type=f32).astype(bf16)
        out[:, frame] = picked.reshape(2 * Y, POSITIONS // (2 * Y), COLS)


def finish_kernel(core, local, c_all, entering, fade, gain, order):
    steps = OWN // COLS
    piece = POSITIONS // (2 * Y)

    def column(i, core):
        return (0, i)

    return pl.pallas_call(
        finish_body,
        out_shape=jax.ShapeDtypeStruct((2 * Y, 2, piece, OWN), bf16),
        grid_spec=pltpu.PrefetchScalarGridSpec(
            num_scalar_prefetch=1,
            grid=(steps,),
            in_specs=[
                pl.BlockSpec((ROWS, COLS), column),
                whole(c_all.shape),
                pl.BlockSpec((Y, COLS // 128 * (STATE // Y), 128), lambda i, core: (0, i, 0)),
                pl.BlockSpec((ROWS, COLS), column),
                pl.BlockSpec((1, COLS), lambda i, core: (0, core[0] * steps + i)),
                whole(order.shape),
            ],
            out_specs=pl.BlockSpec((2 * Y, 2, piece, COLS), lambda i, core: (0, 0, 0, i)),
        ),
        compiler_params=params(),
        name="finish",
    )(core, local, c_all, entering, fade, gain, order)


def regroup_body(part, out):
    row = lax.broadcasted_iota(jnp.int32, (POSITIONS, POSITIONS), 0)
    col = lax.broadcasted_iota(jnp.int32, (POSITIONS, POSITIONS), 1)
    piece = POSITIONS // (2 * Y)
    pick = jnp.where(col == (row % (2 * Y)) * piece + row // (2 * Y), 1.0, 0.0).astype(bf16)
    rows = part[...].reshape(POSITIONS, OWN // 2)
    out[...] = jnp.dot(pick, rows, preferred_element_type=f32).astype(bf16)


def regroup_kernel(part):
    half = OWN // 2
    return pl.pallas_call(
        regroup_body,
        out_shape=jax.ShapeDtypeStruct((POSITIONS, 2 * OWN), bf16),
        grid=(4,),
        in_specs=[
            pl.BlockSpec(
                (Y, None, 2, POSITIONS // (2 * Y), half), lambda i: (0, i // 2, 0, 0, i % 2)
            )
        ],
        out_specs=pl.BlockSpec((POSITIONS, half), lambda i: (0, i)),
        compiler_params=params(),
        name="regroup",
    )(part)


def norm_rows(rows, gain):
    widened = rows.astype(f32)
    inverse = lax.rsqrt(jnp.mean(widened * widened, axis=1, keepdims=True) + EPS)
    return (widened * inverse * gain).astype(bf16)


def norm_body(core, own, sibling, gain, out):
    size = 64

    def one(i, carry):
        at = pl.multiple_of(i * size, size)
        mine = pl.multiple_of(PAD + core[0] * POSITIONS + at, PAD)
        other = pl.multiple_of(PAD + (1 - core[0]) * POSITIONS + at, PAD)
        out[pl.ds(mine, size), :] = norm_rows(own[pl.ds(at, size), :], gain[...])
        out[pl.ds(other, size), :] = norm_rows(sibling[pl.ds(at, size), :], gain[...])
        return carry

    out[:PAD, :] = jnp.zeros((PAD, out.shape[1]), bf16)
    lax.fori_loop(0, POSITIONS // size, one, 0)


def norm_kernel(core, own, sibling, gain):
    width = own.shape[1]
    return pl.pallas_call(
        norm_body,
        out_shape=jax.ShapeDtypeStruct((PAD + ROWS, width), bf16),
        in_specs=[pl.BlockSpec(memory_space=pltpu.SMEM)]
        + [pl.BlockSpec(memory_space=pltpu.VMEM) for _ in range(3)],
        compiler_params=params(),
        name="norm",
    )(core, own, sibling, gain)


def tail_body(rows, gain, normed, out):
    out[...] = norm_rows(rows[...], gain[...])


def tail_kernel(rows, gain, normed):
    return pl.pallas_call(
        tail_body,
        out_shape=jax.ShapeDtypeStruct(normed.shape, bf16),
        grid=(1,),
        in_specs=[whole(rows.shape), whole(gain.shape), pl.BlockSpec(memory_space=pl.ANY)],
        out_specs=pl.BlockSpec(rows.shape, lambda i: (0, 0)),
        input_output_aliases={2: 0},
        compiler_params=params(),
        name="tail",
    )(rows, gain, normed)


def decay_body(core, own, other, cum_r, cum_two, cum_c, step_c, whole_c, fades):
    count = OWN // HEADDIM
    heads = COLS // HEADDIM
    mine = own[pl.ds(pl.multiple_of(core[0] * count, count), count), :]
    earlier = jnp.where(core[0] == 0, mine, other[...])
    later = jnp.where(core[0] == 0, other[...], mine)
    per = POSITIONS // GROUP
    rows = jnp.concatenate(
        [a[:, GROUP * j : GROUP * j + GROUP] for a in (earlier, later) for j in range(per)], axis=0
    )
    row = lax.broadcasted_iota(jnp.int32, (GROUP, GROUP), 0)
    lane = lax.broadcasted_iota(jnp.int32, (GROUP, GROUP), 1)
    upto = jnp.where(row <= lane, 1.0, 0.0).astype(f32)
    cum = jnp.dot(rows, upto, preferred_element_type=f32, precision=lax.Precision.HIGHEST)
    before = [jnp.zeros((count, 1), f32)]
    for j in range(BLOCKS):
        before.append(before[-1] + cum[count * j : count * j + count, GROUP - 1 : GROUP])
    since = cum + jnp.concatenate(before[:BLOCKS], axis=0)
    step = -rows
    log_step = jnp.where(step > 0.0, jnp.log(jnp.where(step > 0.0, step, 1.0)), -1e30)
    two_r = (cum - log_step) * LOG2E
    turned = [a.T for a in (cum * LOG2E, cum, step, since)]
    for i in range(OWN // COLS):
        for j in range(BLOCKS):
            at = slice(GROUP * j, GROUP * j + GROUP)
            some = slice(count * j + heads * i, count * j + heads * i + heads)
            cum_r[i, :, at] = two_r[some, :]
            for out, a in zip((cum_two, cum_c, step_c, whole_c), turned):
                out[i, at, :] = a[:, some]
    fade = jnp.broadcast_to(jnp.exp(before[BLOCKS]), (count, 128))
    first = lax.broadcasted_iota(jnp.int32, (1, 128), 1) < HEADDIM
    pairs = OWN // 128
    spread_out = jnp.concatenate(
        [jnp.where(first, fade[2 * p : 2 * p + 1], fade[2 * p + 1 : 2 * p + 2]) for p in range(pairs)],
        axis=0,
    )
    high = spread_out.astype(bf16).astype(f32)
    fades[...] = jnp.concatenate([high, spread_out - high], axis=0).astype(bf16)


def decay_kernel(core, own, other):
    steps = OWN // COLS
    heads = COLS // HEADDIM
    in_columns = jax.ShapeDtypeStruct((steps, ROWS, heads), f32)
    return pl.pallas_call(
        decay_body,
        out_shape=(
            jax.ShapeDtypeStruct((steps, heads, ROWS), f32),
            in_columns, in_columns, in_columns, in_columns,
            jax.ShapeDtypeStruct((PAD, 128), bf16),
        ),
        in_specs=[pl.BlockSpec(memory_space=pltpu.SMEM)]
        + [pl.BlockSpec(memory_space=pltpu.VMEM) for _ in range(2)],
        compiler_params=params(),
        name="decay",
    )(core, own, other)


def expand_body(cum_c, step_c, whole_c, e_in, e_out, e_all):
    first = lax.broadcasted_iota(jnp.int32, (GROUP, GROUP), 1) < HEADDIM

    def one(j, carry):
        here = pl.ds(pl.multiple_of(j * GROUP, GROUP), GROUP)
        for pair in range(COLS // 128):
            wide = slice(128 * pair, 128 * pair + 128)

            def by_lane(a):
                columns = [
                    jnp.broadcast_to(a[0, here, h : h + 1], (GROUP, GROUP))
                    for h in (2 * pair, 2 * pair + 1)
                ]
                return jnp.where(first, columns[0], columns[1])

            cum = by_lane(cum_c)
            e_in[here, wide] = jnp.exp(cum)
            e_out[here, wide] = jnp.exp(cum[GROUP - 1 :, :] - cum) * by_lane(step_c)
            e_all[here, wide] = jnp.exp(by_lane(whole_c))
        return carry

    lax.fori_loop(0, BLOCKS, one, 0)


def expand_kernel(cum_c, step_c, whole_c):
    steps = OWN // COLS
    heads = COLS // HEADDIM
    return pl.pallas_call(
        expand_body,
        out_shape=(jax.ShapeDtypeStruct((ROWS, OWN), f32),) * 3,
        grid=(steps,),
        in_specs=[pl.BlockSpec((1, ROWS, heads), lambda i: (i, 0, 0))] * 3,
        out_specs=(pl.BlockSpec((ROWS, COLS), lambda i: (0, i)),) * 3,
        compiler_params=params(),
        name="expand",
    )(cum_c, step_c, whole_c)


def on_device(
    tokens, in_gain, in_weight, conv_weight, conv_bias, log_decay, skip, out_gain, scan_order
):
    seq = lax.axis_index("seq")
    core = seq % 2
    y = seq // 2
    swap = [(i, i ^ 1) for i in range(2 * Y)]
    onward = [(i, i + 2) for i in range(2 * Y - 2)]
    head_count = OWN // HEADDIM
    which = core.astype(jnp.int32)[None]

    weight = jnp.concatenate(
        [in_weight[:, 2 * OWN :], lax.dynamic_slice_in_dim(in_weight, core * OWN, OWN, 1)], axis=1
    )
    half = lax.dynamic_slice_in_dim(weight, (y % 2) * 32, 32, 0)
    far = spread(half, far_groups()).reshape(128, 2 * STATE + OWN)
    starts = [sum(PARTS[:g]) for g in range(len(PARTS) + 1)]
    cuts = [0] + [2 * STATE + COLS * start for start in starts[1:]]
    far_chunks = [far[:, a:b] for a, b in zip(cuts, cuts[1:])]
    chunks = [spread(far_chunks[0], near_groups())]

    own = tokens[0]
    gain = in_gain[None, :]
    sibling = lax.ppermute(own, "seq", swap)
    tail = jnp.where(core == 1, own[POSITIONS - PAD :], sibling[POSITIONS - PAD :])
    tail = lax.ppermute(tail, "seq", onward)
    normed = norm_kernel(which, own, sibling, gain)
    other = lax.dynamic_slice_in_dim(log_decay[0], (1 - core) * head_count, head_count, 0)
    cum_r, cum_two, cum_c, step_c, whole_c, fades = decay_kernel(
        which, log_decay[0], lax.ppermute(other, "seq", swap)
    )
    decays = (cum_r, cum_two, fades) + tuple(expand_kernel(cum_c, step_c, whole_c))
    bias = conv_bias[None, :]
    last_gain = out_gain[None, :]
    order = scan_order[:, None]

    normed, tail, decays, bias, last_gain, order, far_chunks = lax.optimization_barrier(
        (normed, tail, decays, bias, last_gain, order, far_chunks)
    )
    cum_r, cum_two, fades, e_in, e_out, e_all = decays
    normed = tail_kernel(tail, gain, normed)
    chunks.append(spread(far_chunks[1], near_groups()))

    b_all, c_all, scores = bc_kernel(normed, chunks[0], conv_weight, bias)
    same_core = [list(range(c, 2 * Y, 2)) for c in range(2)]
    earlier = ()
    for g, steps in enumerate(PARTS):
        earlier = heads_kernel(
            which, starts[g], steps, normed, chunks[g], 1 if g == 0 else 0, conv_weight, bias,
            b_all, c_all, scores, cum_two, cum_r, e_in, e_out, skip, fades, earlier,
        )
        if g + 2 < len(PARTS):
            following, sent = lax.optimization_barrier((far_chunks[g + 2], earlier[1]))
            earlier = (earlier[0], sent)
            chunks.append(spread(following, near_groups()))
    local, sent = earlier
    parts = lax.all_to_all(sent, "seq", 0, 0, axis_index_groups=same_core, tiled=True)
    entering = lax.all_to_all(
        chain_kernel(parts), "seq", 0, 0, axis_index_groups=same_core, tiled=True
    )
    outgoing = finish_kernel(which, local, c_all, entering, e_all, last_gain, order)
    back = lax.all_to_all(outgoing, "seq", 0, 0, tiled=True)
    return regroup_kernel(back.reshape(Y, 2, 2, POSITIONS // (2 * Y), OWN))[None]


def solution(mesh):
    in_specs = (
        P("dp", "seq", None),
        P(),
        P("dp", None),
        P(),
        P(),
        P("dp", None, "seq"),
        P(),
        P(),
        P(),
    )
    out_specs = P("dp", "seq", None)
    return jax.shard_map(
        on_device, mesh=mesh, in_specs=in_specs, out_specs=out_specs, check_vma=False
    )
```

```python
import functools

import jax
import jax.numpy as jnp
from jax import lax
from jax.experimental import pallas as pl
from jax.experimental.pallas import tpu as pltpu
from jax.sharding import PartitionSpec as P

HEADDIM = 64
STATE = 128
GROUP = 128
POSITIONS = 512
ROWS = 1024
PAD = 16
BLOCKS = ROWS // GROUP
OWN = 1024
COLS = 256
PARTS = (2, 2)
LOG2E = 1.4426950408889634
EPS = 1e-05

Z, X, Y = 8, 4, 8
bf16 = jnp.bfloat16
f32 = jnp.float32


def place(z, x, y, core):
    return (z * X + x) * (2 * Y) + 2 * y + core


def far_groups():
    return [
        [place(2 * k + dz, x, y, c) for k in range(Z // 2)]
        for dz in range(2)
        for x in range(X)
        for y in range(Y)
        for c in range(2)
    ]


def near_groups():
    return [
        [place(2 * zp + dz, x, 2 * yp + dy, c) for dz in range(2) for x in range(X) for dy in range(2)]
        for zp in range(Z // 2)
        for yp in range(Y // 2)
        for c in range(2)
    ]


def spread(block, groups):
    count = len(groups[0])
    return lax.all_to_all(
        jnp.broadcast_to(block[None], (count,) + block.shape),
        ("dp", "seq"), 0, 0, axis_index_groups=groups, tiled=True,
    )


def params():
    return pltpu.CompilerParams(vmem_limit_bytes=58 * 1024 * 1024)


def whole(shape):
    return pl.BlockSpec(shape, lambda *_: (0,) * len(shape))


def project(normed, w, w_all, p_all):
    for k in range(4):
        w_all[512 * k : 512 * k + 512, :] = w[:, 32 * k : 32 * k + 32, :].reshape(512, w.shape[2])
    p_all[...] = (
        jnp.dot(normed[...], w_all[...], preferred_element_type=f32).astype(bf16).astype(f32)
    )


def mixed_rows(start, taps, bias, p_all):
    rows = p_all.at[pl.ds(pl.multiple_of(start + 8, 8), GROUP + 8), :]
    pre = bias[...] + taps[0:1, :] * rows[5 : 5 + GROUP, :]
    for k in range(1, 4):
        pre = pre + taps[k : k + 1, :] * rows[5 + k : 5 + k + GROUP, :]
    half = 0.5 * pre
    return (half + half * jnp.tanh(half)).astype(bf16)


def bc_body(core, normed, w, taps, bias, out, w_all, p_all):
    project(normed, w, w_all, p_all)

    def one(j, carry):
        start = pl.multiple_of(j * GROUP, GROUP)
        out[pl.ds(start, GROUP), :] = mixed_rows(start, taps, bias, p_all)
        return carry

    lax.fori_loop(0, BLOCKS, one, 0)


def bc_kernel(core, normed, w, taps, bias):
    last = w.shape[2] // STATE - 1

    def channels(i, core):
        return (0, 2 * OWN // STATE + core[0])

    return pl.pallas_call(
        bc_body,
        out_shape=jax.ShapeDtypeStruct((ROWS, STATE), bf16),
        grid_spec=pltpu.PrefetchScalarGridSpec(
            num_scalar_prefetch=1,
            grid=(1,),
            in_specs=[
                whole(normed.shape),
                pl.BlockSpec((16, 128, STATE), lambda i, core: (0, 0, last)),
                pl.BlockSpec((4, STATE), channels),
                pl.BlockSpec((1, STATE), channels),
            ],
            out_specs=whole((ROWS, STATE)),
            scratch_shapes=[pltpu.VMEM((2048, STATE), bf16), pltpu.VMEM((PAD + ROWS, STATE), f32)],
        ),
        compiler_params=params(),
        name="bc",
    )(core, normed, w, taps, bias)


def turned_to(columns, step):
    return pltpu.roll(columns, lax.rem(128 - step * (COLS // HEADDIM), 128), 1)


def heads_body(
    base, core, normed, w, taps, bias, b_all, c_all, columns, cum_r, skip, fades, *refs,
):
    local, sent, w_all, p_all, state = refs[-5:]
    i = pl.program_id(0)

    @pl.when(i == 0)
    def _():
        if base:
            sent[...] = refs[1][...]
        else:
            for y in range(Y):
                sent[y, sent.shape[1] - PAD :, :] = fades[...]

    project(normed, w, w_all, p_all)
    state[...] = jnp.zeros_like(state)
    heads = COLS // HEADDIM
    pairs = COLS // 128
    head = core[0] * (OWN // HEADDIM) + (base + i) * heads
    row = lax.broadcasted_iota(jnp.int32, (GROUP, GROUP), 0)
    lane = lax.broadcasted_iota(jnp.int32, (GROUP, GROUP), 1)
    causal = lane <= row
    first = lane < HEADDIM

    def one(j, carry):
        start = pl.multiple_of(j * GROUP, GROUP)
        here = pl.ds(start, GROUP)
        mixed = mixed_rows(start, taps, bias, p_all)
        b = b_all[here, :]
        c = c_all[here, :]
        scores = lax.dot_general(c, b, (((1,), (1,)), ((), ())), preferred_element_type=f32)
        cols = turned_to(columns[here, :], base + i)

        def by_row(h):
            return jnp.broadcast_to(cols[:, h : h + 1], (GROUP, GROUP))

        for pair in range(pairs):
            wide = slice(128 * pair, 128 * pair + 128)
            x = mixed[:, wide].astype(f32)
            weights, cums = [], []
            for h in (2 * pair, 2 * pair + 1):
                cum = by_row(h)
                cums.append(cum)
                gap = cum - cum_r[0, h : h + 1, here]
                weights.append((scores * jnp.exp2(jnp.where(causal, gap, -1e30))).astype(bf16))
            both = jnp.concatenate(weights, axis=1)
            apart = jnp.concatenate(
                [jnp.where(first, x, 0.0).astype(bf16), jnp.where(first, 0.0, x).astype(bf16)], axis=0
            )
            intra = jnp.dot(both, apart, preferred_element_type=f32)
            cum = jnp.where(first, cums[0], cums[1])
            rest = jnp.where(first, by_row(16 + 2 * pair), by_row(17 + 2 * pair))
            scaled = (jnp.exp2(cum[GROUP - 1 :, :] - rest) * x).astype(bf16)
            block_state = lax.dot_general(
                b, scaled, (((0,), (0,)), ((), ())), preferred_element_type=f32
            )
            entering = state[pair]
            fade = jnp.exp2(cum)
            inter = fade * jnp.dot(c, entering.astype(bf16), preferred_element_type=f32)
            gains = jnp.where(first, skip[head + 2 * pair], skip[head + 2 * pair + 1])
            local[here, wide] = (intra + inter + gains * x).astype(bf16)
            state[pair] = fade[GROUP - 1 :, :] * entering + block_state
        return carry

    lax.fori_loop(0, BLOCKS, one, 0)
    slab = STATE // Y
    for y in range(Y):
        for pair in range(pairs):
            at = pl.multiple_of(((base + i) * pairs + pair) * slab, slab)
            sent[y, pl.ds(at, slab), :] = state[pair, slab * y : slab * y + slab, :].astype(bf16)


def heads_kernel(
    core, base, steps, normed, w, taps, bias, bc, columns, cum_r, skip, fades, earlier,
):
    heads = COLS // HEADDIM
    sent = (Y, OWN // 128 * (STATE // Y) + PAD, 128)

    def channels(i, core):
        return (0, core[0] * (OWN // COLS) + base + i)

    def step(i, core):
        return (base + i, 0, 0)

    return pl.pallas_call(
        functools.partial(heads_body, base),
        out_shape=(
            jax.ShapeDtypeStruct((ROWS, OWN), bf16),
            jax.ShapeDtypeStruct(sent, bf16),
        ),
        grid_spec=pltpu.PrefetchScalarGridSpec(
            num_scalar_prefetch=1,
            grid=(steps,),
            in_specs=[
                whole(normed.shape),
                pl.BlockSpec((16, 128, COLS), lambda i, core: (0, 0, i)),
                pl.BlockSpec((4, COLS), channels),
                pl.BlockSpec((1, COLS), channels),
                pl.BlockSpec((None, ROWS, STATE), lambda i, core: (core[0], 0, 0)),
                pl.BlockSpec((None, ROWS, STATE), lambda i, core: (1 - core[0], 0, 0)),
                whole(columns.shape),
                pl.BlockSpec((1, heads, ROWS), step),
                pl.BlockSpec(memory_space=pltpu.SMEM),
                whole(fades.shape),
            ]
            + ([pl.BlockSpec(memory_space=pl.ANY), whole(sent)] if earlier else []),
            out_specs=(
                pl.BlockSpec((ROWS, COLS), lambda i, core: (0, base + i)),
                whole(sent),
            ),
            scratch_shapes=[
                pltpu.VMEM((2048, COLS), bf16),
                pltpu.VMEM((PAD + ROWS, COLS), f32),
                pltpu.VMEM((COLS // 128, STATE, 128), f32),
            ],
        ),
        input_output_aliases={11: 0, 12: 1} if earlier else {},
        compiler_params=params(),
        name="heads",
    )(
        core, normed, w, taps, bias, bc, bc, columns, cum_r, skip, fades, *earlier,
    )


def chain_body(parts, out):
    slab = STATE // Y
    pairs = OWN // 128
    base = pairs * slab
    for pair in range(pairs):
        rows = slice(pair * slab, pair * slab + slab)
        entering = jnp.zeros((slab, 128), f32)
        for y in range(Y):
            out[y, rows, :] = entering.astype(bf16)
            fades = parts[y, base:, :].astype(f32)
            fade = fades[pair : pair + 1] + fades[pairs + pair : pairs + pair + 1]
            entering = fade * entering + parts[y, rows, :].astype(f32)


def chain_kernel(parts):
    return pl.pallas_call(
        chain_body,
        out_shape=jax.ShapeDtypeStruct((Y, parts.shape[1] - PAD, 128), bf16),
        compiler_params=params(),
        name="chain",
    )(parts)


def finish_body(core, local, c_all, entering, columns, gain, order, out):
    lane = lax.broadcasted_iota(jnp.int32, (GROUP, GROUP), 1)
    row = lax.broadcasted_iota(jnp.int32, (GROUP, GROUP), 0)
    same_head = jnp.where((lane < HEADDIM) == (row < HEADDIM), 1.0 / HEADDIM, 0.0).astype(bf16)
    position = lax.broadcasted_iota(jnp.int32, (POSITIONS, POSITIONS), 1)
    pick = jnp.where(position == order[...], 1.0, 0.0).astype(bf16)
    first = lax.broadcasted_iota(jnp.int32, (1, 128), 1) < HEADDIM
    for frame in range(ROWS // POSITIONS):
        here = slice(frame * POSITIONS, (frame + 1) * POSITIONS)
        parts = []
        cols = jnp.exp2(turned_to(columns[here, :], pl.program_id(0)))
        for pair in range(COLS // 128):
            wide = slice(128 * pair, 128 * pair + 128)
            state = entering[:, pair * (STATE // Y) : (pair + 1) * (STATE // Y), :].reshape(STATE, 128)
            inter = jnp.dot(c_all[here, :], state, preferred_element_type=f32)
            h = 32 + 2 * pair
            fade = jnp.where(first, cols[:, h : h + 1], cols[:, h + 1 : h + 2])
            ssm = local[here, wide].astype(f32) + fade * inter
            square = ssm * ssm
            high = square.astype(bf16)
            low = (square - high.astype(f32)).astype(bf16)
            mean = jnp.dot(high, same_head, preferred_element_type=f32) + jnp.dot(
                low, same_head, preferred_element_type=f32
            )
            parts.append((ssm * lax.rsqrt(mean + EPS) * gain[:, wide]).astype(bf16))
        normalized = jnp.concatenate(parts, axis=1)
        picked = jnp.dot(pick, normalized, preferred_element_type=f32).astype(bf16)
        out[:, frame] = picked.reshape(2 * Y, POSITIONS // (2 * Y), COLS)


def finish_kernel(core, local, bc, entering, columns, gain, order):
    steps = OWN // COLS
    piece = POSITIONS // (2 * Y)

    def column(i, core):
        return (0, i)

    return pl.pallas_call(
        finish_body,
        out_shape=jax.ShapeDtypeStruct((2 * Y, 2, piece, OWN), bf16),
        grid_spec=pltpu.PrefetchScalarGridSpec(
            num_scalar_prefetch=1,
            grid=(steps,),
            in_specs=[
                pl.BlockSpec((ROWS, COLS), column),
                pl.BlockSpec((None, ROWS, STATE), lambda i, core: (1 - core[0], 0, 0)),
                pl.BlockSpec((Y, COLS // 128 * (STATE // Y), 128), lambda i, core: (0, i, 0)),
                whole(columns.shape),
                pl.BlockSpec((1, COLS), lambda i, core: (0, core[0] * steps + i)),
                whole(order.shape),
            ],
            out_specs=pl.BlockSpec((2 * Y, 2, piece, COLS), lambda i, core: (0, 0, 0, i)),
        ),
        compiler_params=params(),
        name="finish",
    )(core, local, bc, entering, columns, gain, order)


def regroup_body(part, out):
    row = lax.broadcasted_iota(jnp.int32, (POSITIONS, POSITIONS), 0)
    col = lax.broadcasted_iota(jnp.int32, (POSITIONS, POSITIONS), 1)
    piece = POSITIONS // (2 * Y)
    pick = jnp.where(col == (row % (2 * Y)) * piece + row // (2 * Y), 1.0, 0.0).astype(bf16)
    rows = part[...].reshape(POSITIONS, OWN // 2)
    out[...] = jnp.dot(pick, rows, preferred_element_type=f32).astype(bf16)


def regroup_kernel(part):
    half = OWN // 2
    return pl.pallas_call(
        regroup_body,
        out_shape=jax.ShapeDtypeStruct((POSITIONS, 2 * OWN), bf16),
        grid=(4,),
        in_specs=[
            pl.BlockSpec(
                (Y, None, 2, POSITIONS // (2 * Y), half), lambda i: (0, i // 2, 0, 0, i % 2)
            )
        ],
        out_specs=pl.BlockSpec((POSITIONS, half), lambda i: (0, i)),
        compiler_params=params(),
        name="regroup",
    )(part)


def norm_rows(rows, gain):
    widened = rows.astype(f32)
    inverse = lax.rsqrt(jnp.mean(widened * widened, axis=1, keepdims=True) + EPS)
    return (widened * inverse * gain).astype(bf16)


def norm_body(core, own, sibling, gain, out):
    size = 64

    def one(i, carry):
        at = pl.multiple_of(i * size, size)
        mine = pl.multiple_of(PAD + core[0] * POSITIONS + at, PAD)
        other = pl.multiple_of(PAD + (1 - core[0]) * POSITIONS + at, PAD)
        out[pl.ds(mine, size), :] = norm_rows(own[pl.ds(at, size), :], gain[...])
        out[pl.ds(other, size), :] = norm_rows(sibling[pl.ds(at, size), :], gain[...])
        return carry

    out[:PAD, :] = jnp.zeros((PAD, out.shape[1]), bf16)
    lax.fori_loop(0, POSITIONS // size, one, 0)


def norm_kernel(core, own, sibling, gain):
    width = own.shape[1]
    return pl.pallas_call(
        norm_body,
        out_shape=jax.ShapeDtypeStruct((PAD + ROWS, width), bf16),
        in_specs=[pl.BlockSpec(memory_space=pltpu.SMEM)]
        + [pl.BlockSpec(memory_space=pltpu.VMEM) for _ in range(3)],
        compiler_params=params(),
        name="norm",
    )(core, own, sibling, gain)


def tail_body(rows, gain, normed, out):
    out[...] = norm_rows(rows[...], gain[...])


def tail_kernel(rows, gain, normed):
    return pl.pallas_call(
        tail_body,
        out_shape=jax.ShapeDtypeStruct(normed.shape, bf16),
        grid=(1,),
        in_specs=[whole(rows.shape), whole(gain.shape), pl.BlockSpec(memory_space=pl.ANY)],
        out_specs=pl.BlockSpec(rows.shape, lambda i: (0, 0)),
        input_output_aliases={2: 0},
        compiler_params=params(),
        name="tail",
    )(rows, gain, normed)


def decay_body(core, own, other, cum_r, columns, fades):
    count = OWN // HEADDIM
    heads = COLS // HEADDIM
    mine = own[pl.ds(pl.multiple_of(core[0] * count, count), count), :]
    earlier = jnp.where(core[0] == 0, mine, other[...])
    later = jnp.where(core[0] == 0, other[...], mine)
    per = POSITIONS // GROUP
    rows = jnp.concatenate(
        [a[:, GROUP * j : GROUP * j + GROUP] for a in (earlier, later) for j in range(per)], axis=0
    )
    row = lax.broadcasted_iota(jnp.int32, (GROUP, GROUP), 0)
    lane = lax.broadcasted_iota(jnp.int32, (GROUP, GROUP), 1)
    upto = jnp.where(row <= lane, 1.0, 0.0).astype(f32)
    cum = jnp.dot(rows, upto, preferred_element_type=f32, precision=lax.Precision.HIGHEST)
    before = [jnp.zeros((count, 1), f32)]
    for j in range(BLOCKS):
        before.append(before[-1] + cum[count * j : count * j + count, GROUP - 1 : GROUP])
    since = cum + jnp.concatenate(before[:BLOCKS], axis=0)
    step = -rows
    log_step = jnp.where(step > 0.0, jnp.log(jnp.where(step > 0.0, step, 1.0)), -1e30)
    two_r = (cum - log_step) * LOG2E
    turned = [a.T for a in (cum * LOG2E, two_r, since * LOG2E)]
    fill = jnp.zeros((GROUP, 128 - 3 * count), f32)
    for j in range(BLOCKS):
        some = slice(count * j, count * j + count)
        columns[GROUP * j : GROUP * j + GROUP, :] = jnp.concatenate(
            [a[:, some] for a in turned] + [fill], axis=1
        )
    for i in range(OWN // COLS):
        for j in range(BLOCKS):
            at = slice(GROUP * j, GROUP * j + GROUP)
            some = slice(count * j + heads * i, count * j + heads * i + heads)
            cum_r[i, :, at] = two_r[some, :]
    fade = jnp.broadcast_to(jnp.exp(before[BLOCKS]), (count, 128))
    first = lax.broadcasted_iota(jnp.int32, (1, 128), 1) < HEADDIM
    pairs = OWN // 128
    spread_out = jnp.concatenate(
        [jnp.where(first, fade[2 * p : 2 * p + 1], fade[2 * p + 1 : 2 * p + 2]) for p in range(pairs)],
        axis=0,
    )
    high = spread_out.astype(bf16).astype(f32)
    fades[...] = jnp.concatenate([high, spread_out - high], axis=0).astype(bf16)


def decay_kernel(core, own, other):
    steps = OWN // COLS
    heads = COLS // HEADDIM
    return pl.pallas_call(
        decay_body,
        out_shape=(
            jax.ShapeDtypeStruct((steps, heads, ROWS), f32),
            jax.ShapeDtypeStruct((ROWS, 128), f32),
            jax.ShapeDtypeStruct((PAD, 128), bf16),
        ),
        in_specs=[pl.BlockSpec(memory_space=pltpu.SMEM)]
        + [pl.BlockSpec(memory_space=pltpu.VMEM) for _ in range(2)],
        compiler_params=params(),
        name="decay",
    )(core, own, other)


def on_device(
    tokens, in_gain, in_weight, conv_weight, conv_bias, log_decay, skip, out_gain, scan_order
):
    seq = lax.axis_index("seq")
    core = seq % 2
    y = seq // 2
    swap = [(i, i ^ 1) for i in range(2 * Y)]
    onward = [(i, i + 2) for i in range(2 * Y - 2)]
    head_count = OWN // HEADDIM
    which = core.astype(jnp.int32)[None]

    first_half = sum(PARTS[:1]) * COLS

    def weight_columns(start, count):
        return lax.dynamic_slice_in_dim(in_weight, start, count, 1)

    weight = jnp.concatenate(
        [
            weight_columns(core * OWN, first_half),
            weight_columns(2 * OWN + core * STATE, STATE),
            weight_columns(core * OWN + first_half, OWN - first_half),
        ],
        axis=1,
    )
    half = lax.dynamic_slice_in_dim(weight, (y % 2) * 32, 32, 0)
    far = spread(half, far_groups()).reshape(128, STATE + OWN)
    starts = [sum(PARTS[:g]) for g in range(len(PARTS) + 1)]
    cuts = [0] + [STATE + COLS * start for start in starts[1:]]
    far_chunks = [far[:, a:b] for a, b in zip(cuts, cuts[1:])]
    chunks = [spread(far_chunks[0], near_groups())]

    own = tokens[0]
    gain = in_gain[None, :]
    sibling = lax.ppermute(own, "seq", swap)
    tail = jnp.where(core == 1, own[POSITIONS - PAD :], sibling[POSITIONS - PAD :])
    tail = lax.ppermute(tail, "seq", onward)
    normed = norm_kernel(which, own, sibling, gain)
    other = lax.dynamic_slice_in_dim(log_decay[0], (1 - core) * head_count, head_count, 0)
    decays = decay_kernel(which, log_decay[0], lax.ppermute(other, "seq", swap))
    bias = conv_bias[None, :]
    last_gain = out_gain[None, :]
    order = scan_order[:, None]

    normed, tail, decays, bias, last_gain, order, far_chunks = lax.optimization_barrier(
        (normed, tail, decays, bias, last_gain, order, far_chunks)
    )
    cum_r, columns, fades = decays
    normed = tail_kernel(tail, gain, normed)
    chunks.append(spread(far_chunks[1], near_groups()))

    mine = bc_kernel(which, normed, chunks[0], conv_weight, bias)
    bc = jnp.stack([mine, lax.ppermute(mine, "seq", swap)])
    same_core = [list(range(c, 2 * Y, 2)) for c in range(2)]
    earlier = ()
    for g, steps in enumerate(PARTS):
        earlier = heads_kernel(
            which, starts[g], steps, normed, chunks[g], conv_weight, bias, bc, columns, cum_r, skip,
            fades, earlier,
        )
        if g + 2 < len(PARTS):
            following, sent = lax.optimization_barrier((far_chunks[g + 2], earlier[1]))
            earlier = (earlier[0], sent)
            chunks.append(spread(following, near_groups()))
    local, sent = earlier
    parts = lax.all_to_all(sent, "seq", 0, 0, axis_index_groups=same_core, tiled=True)
    entering = lax.all_to_all(
        chain_kernel(parts), "seq", 0, 0, axis_index_groups=same_core, tiled=True
    )
    outgoing = finish_kernel(which, local, bc, entering, columns, last_gain, order)
    back = lax.all_to_all(outgoing, "seq", 0, 0, tiled=True)
    return regroup_kernel(back.reshape(Y, 2, 2, POSITIONS // (2 * Y), OWN))[None]


def solution(mesh):
    in_specs = (
        P("dp", "seq", None),
        P(),
        P("dp", None),
        P(),
        P(),
        P("dp", None, "seq"),
        P(),
        P(),
        P(),
    )
    out_specs = P("dp", "seq", None)
    return jax.shard_map(
        on_device, mesh=mesh, in_specs=in_specs, out_specs=out_specs, check_vma=False
    )
```

```python
import functools

import jax
import jax.numpy as jnp
from jax import lax
from jax.experimental import pallas as pl
from jax.experimental.pallas import tpu as pltpu
from jax.sharding import PartitionSpec as P

HEADDIM = 64
STATE = 128
GROUP = 128
POSITIONS = 512
ROWS = 1024
PAD = 16
BLOCKS = ROWS // GROUP
OWN = 1024
COLS = 256
PARTS = (2, 2)
LOG2E = 1.4426950408889634
EPS = 1e-05

Z, X, Y = 8, 4, 8
bf16 = jnp.bfloat16
f32 = jnp.float32


def place(z, x, y, core):
    return (z * X + x) * (2 * Y) + 2 * y + core


def far_groups():
    return [
        [place(2 * k + dz, x, y, c) for k in range(Z // 2)]
        for dz in range(2)
        for x in range(X)
        for y in range(Y)
        for c in range(2)
    ]


def near_groups():
    return [
        [place(2 * zp + dz, x, 2 * yp + dy, c) for dz in range(2) for x in range(X) for dy in range(2)]
        for zp in range(Z // 2)
        for yp in range(Y // 2)
        for c in range(2)
    ]


def spread(block, groups):
    count = len(groups[0])
    return lax.all_to_all(
        jnp.broadcast_to(block[None], (count,) + block.shape),
        ("dp", "seq"), 0, 0, axis_index_groups=groups, tiled=True,
    )


def params():
    return pltpu.CompilerParams(vmem_limit_bytes=58 * 1024 * 1024)


def whole(shape):
    return pl.BlockSpec(shape, lambda *_: (0,) * len(shape))


def project(normed, w, w_all, p_all):
    for k in range(4):
        w_all[512 * k : 512 * k + 512, :] = w[:, 32 * k : 32 * k + 32, :].reshape(512, w.shape[2])
    p_all[...] = (
        jnp.dot(normed[...], w_all[...], preferred_element_type=f32).astype(bf16).astype(f32)
    )


def mixed_rows(start, taps, bias, p_all):
    rows = p_all.at[pl.ds(pl.multiple_of(start + 8, 8), GROUP + 8), :]
    pre = bias[...] + taps[0:1, :] * rows[5 : 5 + GROUP, :]
    for k in range(1, 4):
        pre = pre + taps[k : k + 1, :] * rows[5 + k : 5 + k + GROUP, :]
    half = 0.5 * pre
    return (half + half * jnp.tanh(half)).astype(bf16)


def bc_body(core, normed, w, taps, bias, out, w_all, p_all):
    project(normed, w, w_all, p_all)

    def one(j, carry):
        start = pl.multiple_of(j * GROUP, GROUP)
        out[pl.ds(start, GROUP), :] = mixed_rows(start, taps, bias, p_all)
        return carry

    lax.fori_loop(0, BLOCKS, one, 0)


def bc_kernel(core, normed, w, taps, bias):
    last = w.shape[2] // STATE - 1

    def channels(i, core):
        return (0, 2 * OWN // STATE + core[0])

    return pl.pallas_call(
        bc_body,
        out_shape=jax.ShapeDtypeStruct((ROWS, STATE), bf16),
        grid_spec=pltpu.PrefetchScalarGridSpec(
            num_scalar_prefetch=1,
            grid=(1,),
            in_specs=[
                whole(normed.shape),
                pl.BlockSpec((16, 128, STATE), lambda i, core: (0, 0, last)),
                pl.BlockSpec((4, STATE), channels),
                pl.BlockSpec((1, STATE), channels),
            ],
            out_specs=whole((ROWS, STATE)),
            scratch_shapes=[pltpu.VMEM((2048, STATE), bf16), pltpu.VMEM((PAD + ROWS, STATE), f32)],
        ),
        compiler_params=params(),
        name="bc",
    )(core, normed, w, taps, bias)


def turned_to(columns, step):
    return pltpu.roll(columns, lax.rem(128 - step * (COLS // HEADDIM), 128), 1)


def heads_body(
    base, core, normed, w, taps, bias, mine, other, columns, cum_r, skip, fades, *refs,
):
    local, sent, w_all, p_all, state = refs[-5:]
    i = pl.program_id(0)

    @pl.when(i == 0)
    def _():
        if base:
            sent[...] = refs[1][...]
        else:
            for y in range(Y):
                sent[y, sent.shape[1] - PAD :, :] = fades[...]

    project(normed, w, w_all, p_all)
    state[...] = jnp.zeros_like(state)
    heads = COLS // HEADDIM
    pairs = COLS // 128
    head = core[0] * (OWN // HEADDIM) + (base + i) * heads
    row = lax.broadcasted_iota(jnp.int32, (GROUP, GROUP), 0)
    lane = lax.broadcasted_iota(jnp.int32, (GROUP, GROUP), 1)
    causal = lane <= row
    first = lane < HEADDIM

    def one(j, carry):
        start = pl.multiple_of(j * GROUP, GROUP)
        here = pl.ds(start, GROUP)
        mixed = mixed_rows(start, taps, bias, p_all)
        ours, theirs = mine[here, :], other[here, :]
        b = jnp.where(core[0] == 0, ours, theirs)
        c = jnp.where(core[0] == 0, theirs, ours)
        scores = lax.dot_general(c, b, (((1,), (1,)), ((), ())), preferred_element_type=f32)
        cols = turned_to(columns[here, :], base + i)

        def by_row(h):
            return jnp.broadcast_to(cols[:, h : h + 1], (GROUP, GROUP))

        for pair in range(pairs):
            wide = slice(128 * pair, 128 * pair + 128)
            x = mixed[:, wide].astype(f32)
            weights, cums = [], []
            for h in (2 * pair, 2 * pair + 1):
                cum = by_row(h)
                cums.append(cum)
                gap = cum - cum_r[0, h : h + 1, here]
                weights.append((scores * jnp.exp2(jnp.where(causal, gap, -1e30))).astype(bf16))
            both = jnp.concatenate(weights, axis=1)
            apart = jnp.concatenate(
                [jnp.where(first, x, 0.0).astype(bf16), jnp.where(first, 0.0, x).astype(bf16)], axis=0
            )
            intra = jnp.dot(both, apart, preferred_element_type=f32)
            cum = jnp.where(first, cums[0], cums[1])
            rest = jnp.where(first, by_row(16 + 2 * pair), by_row(17 + 2 * pair))
            scaled = (jnp.exp2(cum[GROUP - 1 :, :] - rest) * x).astype(bf16)
            block_state = lax.dot_general(
                b, scaled, (((0,), (0,)), ((), ())), preferred_element_type=f32
            )
            entering = state[pair]
            fade = jnp.exp2(cum)
            inter = fade * jnp.dot(c, entering.astype(bf16), preferred_element_type=f32)
            gains = jnp.where(first, skip[head + 2 * pair], skip[head + 2 * pair + 1])
            local[here, wide] = (intra + inter + gains * x).astype(bf16)
            state[pair] = fade[GROUP - 1 :, :] * entering + block_state
        return carry

    lax.fori_loop(0, BLOCKS, one, 0, unroll=2)
    slab = STATE // Y
    for y in range(Y):
        for pair in range(pairs):
            at = pl.multiple_of(((base + i) * pairs + pair) * slab, slab)
            sent[y, pl.ds(at, slab), :] = state[pair, slab * y : slab * y + slab, :].astype(bf16)


def heads_kernel(
    core, base, steps, normed, w, taps, bias, mine, other, columns, cum_r, skip, fades, earlier,
):
    heads = COLS // HEADDIM
    sent = (Y, OWN // 128 * (STATE // Y) + PAD, 128)

    def channels(i, core):
        return (0, core[0] * (OWN // COLS) + base + i)

    def step(i, core):
        return (base + i, 0, 0)

    return pl.pallas_call(
        functools.partial(heads_body, base),
        out_shape=(
            jax.ShapeDtypeStruct((ROWS, OWN), bf16),
            jax.ShapeDtypeStruct(sent, bf16),
        ),
        grid_spec=pltpu.PrefetchScalarGridSpec(
            num_scalar_prefetch=1,
            grid=(steps,),
            in_specs=[
                whole(normed.shape),
                pl.BlockSpec((16, 128, COLS), lambda i, core: (0, 0, i)),
                pl.BlockSpec((4, COLS), channels),
                pl.BlockSpec((1, COLS), channels),
                whole(mine.shape),
                whole(other.shape),
                whole(columns.shape),
                pl.BlockSpec((1, heads, ROWS), step),
                pl.BlockSpec(memory_space=pltpu.SMEM),
                whole(fades.shape),
            ]
            + ([pl.BlockSpec(memory_space=pl.ANY), whole(sent)] if earlier else []),
            out_specs=(
                pl.BlockSpec((ROWS, COLS), lambda i, core: (0, base + i)),
                whole(sent),
            ),
            scratch_shapes=[
                pltpu.VMEM((2048, COLS), bf16),
                pltpu.VMEM((PAD + ROWS, COLS), f32),
                pltpu.VMEM((COLS // 128, STATE, 128), f32),
            ],
        ),
        input_output_aliases={11: 0, 12: 1} if earlier else {},
        compiler_params=params(),
        name="heads",
    )(
        core, normed, w, taps, bias, mine, other, columns, cum_r, skip, fades, *earlier,
    )


def chain_body(parts, out):
    slab = STATE // Y
    pairs = OWN // 128
    base = pairs * slab
    for pair in range(pairs):
        rows = slice(pair * slab, pair * slab + slab)
        entering = jnp.zeros((slab, 128), f32)
        for y in range(Y):
            out[y, rows, :] = entering.astype(bf16)
            fades = parts[y, base:, :].astype(f32)
            fade = fades[pair : pair + 1] + fades[pairs + pair : pairs + pair + 1]
            entering = fade * entering + parts[y, rows, :].astype(f32)


def chain_kernel(parts):
    return pl.pallas_call(
        chain_body,
        out_shape=jax.ShapeDtypeStruct((Y, parts.shape[1] - PAD, 128), bf16),
        compiler_params=params(),
        name="chain",
    )(parts)


def finish_body(core, local, mine, other, entering, columns, gain, order, out, normalized, pick):
    @pl.when(pl.program_id(0) == 0)
    def _():
        position = lax.broadcasted_iota(jnp.int32, (POSITIONS, POSITIONS), 1)
        pick[...] = jnp.where(position == order[...], 1.0, 0.0).astype(bf16)

    heads = COLS // HEADDIM
    lane = lax.broadcasted_iota(jnp.int32, (GROUP, GROUP), 1)
    row = lax.broadcasted_iota(jnp.int32, (GROUP, GROUP), 0)
    same_head = jnp.where((lane < HEADDIM) == (row < HEADDIM), 1.0 / HEADDIM, 0.0).astype(bf16)
    wanted = 2 * (OWN // HEADDIM) + pl.program_id(0) * heads
    source = lax.broadcasted_iota(jnp.int32, (GROUP, COLS), 0)
    channel = lax.broadcasted_iota(jnp.int32, (GROUP, COLS), 1)
    by_head = jnp.where(source == wanted + channel // HEADDIM, 1.0, 0.0).astype(bf16)
    kept = lane >= 2 * (OWN // HEADDIM)
    states = [
        entering[:, p * (STATE // Y) : (p + 1) * (STATE // Y), :].reshape(STATE, 128)
        for p in range(COLS // 128)
    ]
    state = jnp.concatenate(states, axis=1)

    def one(j, carry):
        here = pl.ds(pl.multiple_of(j * GROUP, GROUP), GROUP)
        fades = jnp.exp2(jnp.where(kept, columns[here, :], 0.0))
        high = fades.astype(bf16)
        low = (fades - high.astype(f32)).astype(bf16)
        fade = jnp.dot(high, by_head, preferred_element_type=f32) + jnp.dot(
            low, by_head, preferred_element_type=f32
        )
        c = jnp.where(core[0] == 0, other[here, :], mine[here, :])
        inter = jnp.dot(c, state, preferred_element_type=f32)
        ssm = local[here, :].astype(f32) + fade * inter
        square = ssm * ssm
        high = square.astype(bf16)
        low = (square - high.astype(f32)).astype(bf16)
        for pair in range(COLS // 128):
            wide = slice(128 * pair, 128 * pair + 128)
            mean = jnp.dot(high[:, wide], same_head, preferred_element_type=f32) + jnp.dot(
                low[:, wide], same_head, preferred_element_type=f32
            )
            scale = lax.rsqrt(mean + EPS) * gain[:, wide]
            normalized[here, wide] = (ssm[:, wide] * scale).astype(bf16)
        return carry

    lax.fori_loop(0, BLOCKS, one, 0, unroll=2)
    for frame in range(ROWS // POSITIONS):
        here = slice(frame * POSITIONS, (frame + 1) * POSITIONS)
        picked = jnp.dot(pick[...], normalized[here, :], preferred_element_type=f32).astype(bf16)
        out[:, frame] = picked.reshape(2 * Y, POSITIONS // (2 * Y), COLS)


def finish_kernel(core, local, mine, other, entering, columns, gain, order):
    steps = OWN // COLS
    piece = POSITIONS // (2 * Y)

    def column(i, core):
        return (0, i)

    return pl.pallas_call(
        finish_body,
        out_shape=jax.ShapeDtypeStruct((2 * Y, 2, piece, OWN), bf16),
        grid_spec=pltpu.PrefetchScalarGridSpec(
            num_scalar_prefetch=1,
            grid=(steps,),
            in_specs=[
                pl.BlockSpec((ROWS, COLS), column),
                whole(mine.shape),
                whole(other.shape),
                pl.BlockSpec((Y, COLS // 128 * (STATE // Y), 128), lambda i, core: (0, i, 0)),
                whole(columns.shape),
                pl.BlockSpec((1, COLS), lambda i, core: (0, core[0] * steps + i)),
                whole(order.shape),
            ],
            out_specs=pl.BlockSpec((2 * Y, 2, piece, COLS), lambda i, core: (0, 0, 0, i)),
            scratch_shapes=[pltpu.VMEM((ROWS, COLS), bf16), pltpu.VMEM((POSITIONS, POSITIONS), bf16)],
        ),
        compiler_params=params(),
        name="finish",
    )(core, local, mine, other, entering, columns, gain, order)


def regroup_body(part, out, pick):
    @pl.when(pl.program_id(0) == 0)
    def _():
        row = lax.broadcasted_iota(jnp.int32, (POSITIONS, POSITIONS), 0)
        col = lax.broadcasted_iota(jnp.int32, (POSITIONS, POSITIONS), 1)
        piece = POSITIONS // (2 * Y)
        chosen = col == (row % (2 * Y)) * piece + row // (2 * Y)
        pick[...] = jnp.where(chosen, 1.0, 0.0).astype(bf16)

    rows = part[...].reshape(POSITIONS, OWN // 2)
    out[...] = jnp.dot(pick[...], rows, preferred_element_type=f32).astype(bf16)


def regroup_kernel(part):
    half = OWN // 2
    return pl.pallas_call(
        regroup_body,
        out_shape=jax.ShapeDtypeStruct((POSITIONS, 2 * OWN), bf16),
        grid=(4,),
        in_specs=[
            pl.BlockSpec(
                (Y, None, 2, POSITIONS // (2 * Y), half), lambda i: (0, i // 2, 0, 0, i % 2)
            )
        ],
        out_specs=pl.BlockSpec((POSITIONS, half), lambda i: (0, i)),
        scratch_shapes=[pltpu.VMEM((POSITIONS, POSITIONS), bf16)],
        compiler_params=params(),
        name="regroup",
    )(part)


def norm_rows(rows, gain):
    widened = rows.astype(f32)
    inverse = lax.rsqrt(jnp.mean(widened * widened, axis=1, keepdims=True) + EPS)
    return (widened * inverse * gain).astype(bf16)


def norm_body(core, own, sibling, gain, out):
    size = 64

    def one(i, carry):
        at = pl.multiple_of(i * size, size)
        mine = pl.multiple_of(PAD + core[0] * POSITIONS + at, PAD)
        other = pl.multiple_of(PAD + (1 - core[0]) * POSITIONS + at, PAD)
        out[pl.ds(mine, size), :] = norm_rows(own[pl.ds(at, size), :], gain[...])
        out[pl.ds(other, size), :] = norm_rows(sibling[pl.ds(at, size), :], gain[...])
        return carry

    out[:PAD, :] = jnp.zeros((PAD, out.shape[1]), bf16)
    lax.fori_loop(0, POSITIONS // size, one, 0)


def norm_kernel(core, own, sibling, gain):
    width = own.shape[1]
    return pl.pallas_call(
        norm_body,
        out_shape=jax.ShapeDtypeStruct((PAD + ROWS, width), bf16),
        in_specs=[pl.BlockSpec(memory_space=pltpu.SMEM)]
        + [pl.BlockSpec(memory_space=pltpu.VMEM) for _ in range(3)],
        compiler_params=params(),
        name="norm",
    )(core, own, sibling, gain)


def tail_body(rows, gain, normed, out):
    out[...] = norm_rows(rows[...], gain[...])


def tail_kernel(rows, gain, normed):
    return pl.pallas_call(
        tail_body,
        out_shape=jax.ShapeDtypeStruct(normed.shape, bf16),
        grid=(1,),
        in_specs=[whole(rows.shape), whole(gain.shape), pl.BlockSpec(memory_space=pl.ANY)],
        out_specs=pl.BlockSpec(rows.shape, lambda i: (0, 0)),
        input_output_aliases={2: 0},
        compiler_params=params(),
        name="tail",
    )(rows, gain, normed)


def decay_body(core, own, other, cum_r, columns, fades):
    count = OWN // HEADDIM
    heads = COLS // HEADDIM
    mine = own[pl.ds(pl.multiple_of(core[0] * count, count), count), :]
    earlier = jnp.where(core[0] == 0, mine, other[...])
    later = jnp.where(core[0] == 0, other[...], mine)
    per = POSITIONS // GROUP
    rows = jnp.concatenate(
        [a[:, GROUP * j : GROUP * j + GROUP] for a in (earlier, later) for j in range(per)], axis=0
    )
    row = lax.broadcasted_iota(jnp.int32, (GROUP, GROUP), 0)
    lane = lax.broadcasted_iota(jnp.int32, (GROUP, GROUP), 1)
    upto = jnp.where(row <= lane, 1.0, 0.0).astype(f32)
    cum = jnp.dot(rows, upto, preferred_element_type=f32, precision=lax.Precision.HIGHEST)
    before = [jnp.zeros((count, 1), f32)]
    for j in range(BLOCKS):
        before.append(before[-1] + cum[count * j : count * j + count, GROUP - 1 : GROUP])
    since = cum + jnp.concatenate(before[:BLOCKS], axis=0)
    step = -rows
    log_step = jnp.where(step > 0.0, jnp.log(jnp.where(step > 0.0, step, 1.0)), -1e30)
    two_r = (cum - log_step) * LOG2E
    turned = [a.T for a in (cum * LOG2E, two_r, since * LOG2E)]
    fill = jnp.zeros((GROUP, 128 - 3 * count), f32)
    for j in range(BLOCKS):
        some = slice(count * j, count * j + count)
        columns[GROUP * j : GROUP * j + GROUP, :] = jnp.concatenate(
            [a[:, some] for a in turned] + [fill], axis=1
        )
    for i in range(OWN // COLS):
        for j in range(BLOCKS):
            at = slice(GROUP * j, GROUP * j + GROUP)
            some = slice(count * j + heads * i, count * j + heads * i + heads)
            cum_r[i, :, at] = two_r[some, :]
    fade = jnp.broadcast_to(jnp.exp(before[BLOCKS]), (count, 128))
    first = lax.broadcasted_iota(jnp.int32, (1, 128), 1) < HEADDIM
    pairs = OWN // 128
    spread_out = jnp.concatenate(
        [jnp.where(first, fade[2 * p : 2 * p + 1], fade[2 * p + 1 : 2 * p + 2]) for p in range(pairs)],
        axis=0,
    )
    high = spread_out.astype(bf16).astype(f32)
    fades[...] = jnp.concatenate([high, spread_out - high], axis=0).astype(bf16)


def decay_kernel(core, own, other):
    steps = OWN // COLS
    heads = COLS // HEADDIM
    return pl.pallas_call(
        decay_body,
        out_shape=(
            jax.ShapeDtypeStruct((steps, heads, ROWS), f32),
            jax.ShapeDtypeStruct((ROWS, 128), f32),
            jax.ShapeDtypeStruct((PAD, 128), bf16),
        ),
        in_specs=[pl.BlockSpec(memory_space=pltpu.SMEM)]
        + [pl.BlockSpec(memory_space=pltpu.VMEM) for _ in range(2)],
        compiler_params=params(),
        name="decay",
    )(core, own, other)


def on_device(
    tokens, in_gain, in_weight, conv_weight, conv_bias, log_decay, skip, out_gain, scan_order
):
    seq = lax.axis_index("seq")
    core = seq % 2
    y = seq // 2
    swap = [(i, i ^ 1) for i in range(2 * Y)]
    onward = [(i, i + 2) for i in range(2 * Y - 2)]
    head_count = OWN // HEADDIM
    which = core.astype(jnp.int32)[None]

    first_half = sum(PARTS[:1]) * COLS

    def weight_columns(start, count):
        return lax.dynamic_slice_in_dim(in_weight, start, count, 1)

    weight = jnp.concatenate(
        [
            weight_columns(core * OWN, first_half),
            weight_columns(2 * OWN + core * STATE, STATE),
            weight_columns(core * OWN + first_half, OWN - first_half),
        ],
        axis=1,
    )
    half = lax.dynamic_slice_in_dim(weight, (y % 2) * 32, 32, 0)
    far = spread(half, far_groups()).reshape(128, STATE + OWN)
    starts = [sum(PARTS[:g]) for g in range(len(PARTS) + 1)]
    cuts = [0] + [STATE + COLS * start for start in starts[1:]]
    far_chunks = [far[:, a:b] for a, b in zip(cuts, cuts[1:])]
    chunks = [spread(far_chunks[0], near_groups())]

    own = tokens[0]
    gain = in_gain[None, :]
    sibling = lax.ppermute(own, "seq", swap)
    tail = jnp.where(core == 1, own[POSITIONS - PAD :], sibling[POSITIONS - PAD :])
    tail = lax.ppermute(tail, "seq", onward)
    normed = norm_kernel(which, own, sibling, gain)
    other = lax.dynamic_slice_in_dim(log_decay[0], (1 - core) * head_count, head_count, 0)
    decays = decay_kernel(which, log_decay[0], lax.ppermute(other, "seq", swap))
    bias = conv_bias[None, :]
    last_gain = out_gain[None, :]
    order = scan_order[:, None]

    normed, tail, decays, bias, last_gain, order, far_chunks = lax.optimization_barrier(
        (normed, tail, decays, bias, last_gain, order, far_chunks)
    )
    cum_r, columns, fades = decays
    normed = tail_kernel(tail, gain, normed)
    chunks.append(spread(far_chunks[1], near_groups()))

    mine = bc_kernel(which, normed, chunks[0], conv_weight, bias)
    theirs = lax.ppermute(mine, "seq", swap)
    same_core = [list(range(c, 2 * Y, 2)) for c in range(2)]
    earlier = ()
    for g, steps in enumerate(PARTS):
        earlier = heads_kernel(
            which, starts[g], steps, normed, chunks[g], conv_weight, bias, mine, theirs, columns, cum_r,
            skip, fades, earlier,
        )
        if g + 2 < len(PARTS):
            following, sent = lax.optimization_barrier((far_chunks[g + 2], earlier[1]))
            earlier = (earlier[0], sent)
            chunks.append(spread(following, near_groups()))
    local, sent = earlier
    parts = lax.all_to_all(sent, "seq", 0, 0, axis_index_groups=same_core, tiled=True)
    entering = lax.all_to_all(
        chain_kernel(parts), "seq", 0, 0, axis_index_groups=same_core, tiled=True
    )
    outgoing = finish_kernel(which, local, mine, theirs, entering, columns, last_gain, order)
    back = lax.all_to_all(outgoing, "seq", 0, 0, tiled=True)
    return regroup_kernel(back.reshape(Y, 2, 2, POSITIONS // (2 * Y), OWN))[None]


def solution(mesh):
    in_specs = (
        P("dp", "seq", None),
        P(),
        P("dp", None),
        P(),
        P(),
        P("dp", None, "seq"),
        P(),
        P(),
        P(),
    )
    out_specs = P("dp", "seq", None)
    return jax.shard_map(
        on_device, mesh=mesh, in_specs=in_specs, out_specs=out_specs, check_vma=False
    )
```

```python
import functools

import jax
import jax.numpy as jnp
from jax import lax
from jax.experimental import pallas as pl
from jax.experimental.pallas import tpu as pltpu
from jax.sharding import PartitionSpec as P

HEADDIM = 64
STATE = 128
GROUP = 128
POSITIONS = 512
ROWS = 1024
PAD = 16
BLOCKS = ROWS // GROUP
OWN = 1024
COLS = 256
PARTS = (2, 2)
LOG2E = 1.4426950408889634
EPS = 1e-05

Z, X, Y = 8, 4, 8
bf16 = jnp.bfloat16
f32 = jnp.float32


def place(z, x, y, core):
    return (z * X + x) * (2 * Y) + 2 * y + core


def far_groups():
    return [
        [place(2 * k + dz, x, y, c) for k in range(Z // 2)]
        for dz in range(2)
        for x in range(X)
        for y in range(Y)
        for c in range(2)
    ]


def near_groups():
    return [
        [place(2 * zp + dz, x, 2 * yp + dy, c) for dz in range(2) for x in range(X) for dy in range(2)]
        for zp in range(Z // 2)
        for yp in range(Y // 2)
        for c in range(2)
    ]


def copies(block, groups):
    return jnp.broadcast_to(block[None], (len(groups[0]),) + block.shape)


def spread(sent, groups):
    return lax.all_to_all(sent, ("dp", "seq"), 0, 0, axis_index_groups=groups, tiled=True)


def params():
    return pltpu.CompilerParams(vmem_limit_bytes=58 * 1024 * 1024)


def whole(shape):
    return pl.BlockSpec(shape, lambda *_: (0,) * len(shape))


def project(normed, w, w_all, p_all):
    for k in range(4):
        w_all[512 * k : 512 * k + 512, :] = w[:, 32 * k : 32 * k + 32, :].reshape(512, w.shape[2])
    p_all[...] = (
        jnp.dot(normed[...], w_all[...], preferred_element_type=f32).astype(bf16).astype(f32)
    )


def mixed_rows(start, taps, bias, p_all):
    rows = p_all.at[pl.ds(pl.multiple_of(start + 8, 8), GROUP + 8), :]
    pre = bias[...] + taps[0:1, :] * rows[5 : 5 + GROUP, :]
    for k in range(1, 4):
        pre = pre + taps[k : k + 1, :] * rows[5 + k : 5 + k + GROUP, :]
    half = 0.5 * pre
    return (half + half * jnp.tanh(half)).astype(bf16)


def bc_body(core, normed, w, taps, bias, out, w_all, p_all):
    project(normed, w, w_all, p_all)

    def one(j, carry):
        start = pl.multiple_of(j * GROUP, GROUP)
        out[pl.ds(start, GROUP), :] = mixed_rows(start, taps, bias, p_all)
        return carry

    lax.fori_loop(0, BLOCKS, one, 0)


def bc_kernel(core, normed, w, taps, bias):
    last = w.shape[2] // STATE - 1

    def channels(i, core):
        return (0, 2 * OWN // STATE + core[0])

    return pl.pallas_call(
        bc_body,
        out_shape=jax.ShapeDtypeStruct((ROWS, STATE), bf16),
        grid_spec=pltpu.PrefetchScalarGridSpec(
            num_scalar_prefetch=1,
            grid=(1,),
            in_specs=[
                whole(normed.shape),
                pl.BlockSpec((16, 128, STATE), lambda i, core: (0, 0, last)),
                pl.BlockSpec((4, STATE), channels),
                pl.BlockSpec((1, STATE), channels),
            ],
            out_specs=whole((ROWS, STATE)),
            scratch_shapes=[pltpu.VMEM((2048, STATE), bf16), pltpu.VMEM((PAD + ROWS, STATE), f32)],
        ),
        compiler_params=params(),
        name="bc",
    )(core, normed, w, taps, bias)


def turned_to(columns, step):
    return pltpu.roll(columns, lax.rem(128 - step * (COLS // HEADDIM), 128), 1)


def heads_body(
    base, core, normed, w, taps, bias, mine, other, columns, cum_r, skip, fades, *refs,
):
    local, sent, w_all, p_all, state = refs[-5:]
    i = pl.program_id(0)

    @pl.when(i == 0)
    def _():
        if base:
            sent[...] = refs[1][...]
        else:
            for y in range(Y):
                sent[y, sent.shape[1] - PAD :, :] = fades[...]

    project(normed, w, w_all, p_all)
    state[...] = jnp.zeros_like(state)
    heads = COLS // HEADDIM
    pairs = COLS // 128
    head = core[0] * (OWN // HEADDIM) + (base + i) * heads
    row = lax.broadcasted_iota(jnp.int32, (GROUP, GROUP), 0)
    lane = lax.broadcasted_iota(jnp.int32, (GROUP, GROUP), 1)
    causal = lane <= row
    first = lane < HEADDIM

    def one(j, carry):
        start = pl.multiple_of(j * GROUP, GROUP)
        here = pl.ds(start, GROUP)
        mixed = mixed_rows(start, taps, bias, p_all)
        ours, theirs = mine[here, :], other[here, :]
        b = jnp.where(core[0] == 0, ours, theirs)
        c = jnp.where(core[0] == 0, theirs, ours)
        scores = lax.dot_general(c, b, (((1,), (1,)), ((), ())), preferred_element_type=f32)
        cols = turned_to(columns[here, :], base + i)

        def by_row(h):
            return jnp.broadcast_to(cols[:, h : h + 1], (GROUP, GROUP))

        for pair in range(pairs):
            wide = slice(128 * pair, 128 * pair + 128)
            x = mixed[:, wide].astype(f32)
            weights, cums = [], []
            for h in (2 * pair, 2 * pair + 1):
                cum = by_row(h)
                cums.append(cum)
                gap = cum - cum_r[0, h : h + 1, here]
                weights.append((scores * jnp.exp2(jnp.where(causal, gap, -1e30))).astype(bf16))
            both = jnp.concatenate(weights, axis=1)
            apart = jnp.concatenate(
                [jnp.where(first, x, 0.0).astype(bf16), jnp.where(first, 0.0, x).astype(bf16)], axis=0
            )
            intra = jnp.dot(both, apart, preferred_element_type=f32)
            cum = jnp.where(first, cums[0], cums[1])
            rest = jnp.where(first, by_row(16 + 2 * pair), by_row(17 + 2 * pair))
            scaled = (jnp.exp2(cum[GROUP - 1 :, :] - rest) * x).astype(bf16)
            block_state = lax.dot_general(
                b, scaled, (((0,), (0,)), ((), ())), preferred_element_type=f32
            )
            entering = state[pair]
            fade = jnp.exp2(cum)
            inter = fade * jnp.dot(c, entering.astype(bf16), preferred_element_type=f32)
            gains = jnp.where(first, skip[head + 2 * pair], skip[head + 2 * pair + 1])
            local[here, wide] = (intra + inter + gains * x).astype(bf16)
            state[pair] = fade[GROUP - 1 :, :] * entering + block_state
        return carry

    lax.fori_loop(0, BLOCKS, one, 0, unroll=4)
    slab = STATE // Y
    for y in range(Y):
        for pair in range(pairs):
            at = pl.multiple_of(((base + i) * pairs + pair) * slab, slab)
            sent[y, pl.ds(at, slab), :] = state[pair, slab * y : slab * y + slab, :].astype(bf16)


def heads_kernel(
    core, base, steps, normed, w, taps, bias, mine, other, columns, cum_r, skip, fades, earlier,
):
    heads = COLS // HEADDIM
    sent = (Y, OWN // 128 * (STATE // Y) + PAD, 128)

    def channels(i, core):
        return (0, core[0] * (OWN // COLS) + base + i)

    def step(i, core):
        return (base + i, 0, 0)

    return pl.pallas_call(
        functools.partial(heads_body, base),
        out_shape=(
            jax.ShapeDtypeStruct((ROWS, OWN), bf16),
            jax.ShapeDtypeStruct(sent, bf16),
        ),
        grid_spec=pltpu.PrefetchScalarGridSpec(
            num_scalar_prefetch=1,
            grid=(steps,),
            in_specs=[
                whole(normed.shape),
                pl.BlockSpec((16, 128, COLS), lambda i, core: (0, 0, i)),
                pl.BlockSpec((4, COLS), channels),
                pl.BlockSpec((1, COLS), channels),
                whole(mine.shape),
                whole(other.shape),
                whole(columns.shape),
                pl.BlockSpec((1, heads, ROWS), step),
                pl.BlockSpec(memory_space=pltpu.SMEM),
                whole(fades.shape),
            ]
            + ([pl.BlockSpec(memory_space=pl.ANY), whole(sent)] if earlier else []),
            out_specs=(
                pl.BlockSpec((ROWS, COLS), lambda i, core: (0, base + i)),
                whole(sent),
            ),
            scratch_shapes=[
                pltpu.VMEM((2048, COLS), bf16),
                pltpu.VMEM((PAD + ROWS, COLS), f32),
                pltpu.VMEM((COLS // 128, STATE, 128), f32),
            ],
        ),
        input_output_aliases={11: 0, 12: 1} if earlier else {},
        compiler_params=params(),
        name="heads",
    )(
        core, normed, w, taps, bias, mine, other, columns, cum_r, skip, fades, *earlier,
    )


def chain_body(parts, out):
    slab = STATE // Y
    pairs = OWN // 128
    base = pairs * slab
    for pair in range(pairs):
        rows = slice(pair * slab, pair * slab + slab)
        entering = jnp.zeros((slab, 128), f32)
        for y in range(Y):
            out[y, rows, :] = entering.astype(bf16)
            fades = parts[y, base:, :].astype(f32)
            fade = fades[pair : pair + 1] + fades[pairs + pair : pairs + pair + 1]
            entering = fade * entering + parts[y, rows, :].astype(f32)


def chain_kernel(parts):
    return pl.pallas_call(
        chain_body,
        out_shape=jax.ShapeDtypeStruct((Y, parts.shape[1] - PAD, 128), bf16),
        compiler_params=params(),
        name="chain",
    )(parts)


def finish_body(core, local, mine, other, entering, columns, gain, order, out, pick):
    @pl.when(pl.program_id(0) == 0)
    def _():
        position = lax.broadcasted_iota(jnp.int32, (POSITIONS, POSITIONS), 1)
        pick[...] = jnp.where(position == order[...], 1.0, 0.0).astype(bf16)

    heads = COLS // HEADDIM
    row = lax.broadcasted_iota(jnp.int32, (COLS, COLS), 0)
    lane = lax.broadcasted_iota(jnp.int32, (COLS, COLS), 1)
    same_head = jnp.where(row // HEADDIM == lane // HEADDIM, 1.0 / HEADDIM, 0.0).astype(bf16)
    wanted = 2 * (OWN // HEADDIM) + pl.program_id(0) * heads
    source = lax.broadcasted_iota(jnp.int32, (GROUP, COLS), 0)
    channel = lax.broadcasted_iota(jnp.int32, (GROUP, COLS), 1)
    by_head = jnp.where(source == wanted + channel // HEADDIM, 1.0, 0.0).astype(bf16)
    kept = lax.broadcasted_iota(jnp.int32, (1, GROUP), 1) >= 2 * (OWN // HEADDIM)
    states = [
        entering[:, p * (STATE // Y) : (p + 1) * (STATE // Y), :].reshape(STATE, 128)
        for p in range(COLS // 128)
    ]
    state = jnp.concatenate(states, axis=1)

    for frame in range(ROWS // POSITIONS):
        here = slice(frame * POSITIONS, (frame + 1) * POSITIONS)
        fades = jnp.exp2(jnp.where(kept, columns[here, :], 0.0))
        high = fades.astype(bf16)
        low = (fades - high.astype(f32)).astype(bf16)
        fade = jnp.dot(high, by_head, preferred_element_type=f32) + jnp.dot(
            low, by_head, preferred_element_type=f32
        )
        c = jnp.where(core[0] == 0, other[here, :], mine[here, :])
        inter = jnp.dot(c, state, preferred_element_type=f32)
        ssm = local[here, :].astype(f32) + fade * inter
        mean = jnp.dot((ssm * ssm).astype(bf16), same_head, preferred_element_type=f32)
        normalized = (ssm * lax.rsqrt(mean + EPS) * gain[...]).astype(bf16)
        picked = jnp.dot(pick[...], normalized, preferred_element_type=f32).astype(bf16)
        out[:, frame] = picked.reshape(2 * Y, POSITIONS // (2 * Y), COLS)


def finish_kernel(core, local, mine, other, entering, columns, gain, order):
    steps = OWN // COLS
    piece = POSITIONS // (2 * Y)

    def column(i, core):
        return (0, i)

    return pl.pallas_call(
        finish_body,
        out_shape=jax.ShapeDtypeStruct((2 * Y, 2, piece, OWN), bf16),
        grid_spec=pltpu.PrefetchScalarGridSpec(
            num_scalar_prefetch=1,
            grid=(steps,),
            in_specs=[
                pl.BlockSpec((ROWS, COLS), column),
                whole(mine.shape),
                whole(other.shape),
                pl.BlockSpec((Y, COLS // 128 * (STATE // Y), 128), lambda i, core: (0, i, 0)),
                whole(columns.shape),
                pl.BlockSpec((1, COLS), lambda i, core: (0, core[0] * steps + i)),
                whole(order.shape),
            ],
            out_specs=pl.BlockSpec((2 * Y, 2, piece, COLS), lambda i, core: (0, 0, 0, i)),
            scratch_shapes=[pltpu.VMEM((POSITIONS, POSITIONS), bf16)],
        ),
        compiler_params=params(),
        name="finish",
    )(core, local, mine, other, entering, columns, gain, order)


def regroup_body(part, out, pick):
    frames = 2 * Y

    @pl.when(pl.program_id(0) == 0)
    def _():
        row = lax.broadcasted_iota(jnp.int32, pick.shape, 0)
        col = lax.broadcasted_iota(jnp.int32, pick.shape, 1)
        each = pick.shape[0] // frames
        pick[...] = jnp.where(col == (row % frames) * each + row // frames, 1.0, 0.0).astype(bf16)

    rows = part[...].reshape(pick.shape[0], OWN)
    out[...] = jnp.dot(pick[...], rows, preferred_element_type=f32).astype(bf16)


def regroup_kernel(part):
    each = POSITIONS // (2 * Y) // 2
    rows = POSITIONS // 2
    return pl.pallas_call(
        regroup_body,
        out_shape=jax.ShapeDtypeStruct((POSITIONS, 2 * OWN), bf16),
        grid=(4,),
        in_specs=[pl.BlockSpec((Y, None, 2, each, OWN), lambda i: (0, i % 2, 0, i // 2, 0))],
        out_specs=pl.BlockSpec((rows, OWN), lambda i: (i // 2, i % 2)),
        scratch_shapes=[pltpu.VMEM((rows, rows), bf16)],
        compiler_params=params(),
        name="regroup",
    )(part)


def norm_rows(rows, gain):
    widened = rows.astype(f32)
    inverse = lax.rsqrt(jnp.mean(widened * widened, axis=1, keepdims=True) + EPS)
    return (widened * inverse * gain).astype(bf16)


def norm_body(core, own, sibling, gain, out):
    size = 64

    def one(i, carry):
        at = pl.multiple_of(i * size, size)
        mine = pl.multiple_of(PAD + core[0] * POSITIONS + at, PAD)
        other = pl.multiple_of(PAD + (1 - core[0]) * POSITIONS + at, PAD)
        out[pl.ds(mine, size), :] = norm_rows(own[pl.ds(at, size), :], gain[...])
        out[pl.ds(other, size), :] = norm_rows(sibling[pl.ds(at, size), :], gain[...])
        return carry

    out[:PAD, :] = jnp.zeros((PAD, out.shape[1]), bf16)
    lax.fori_loop(0, POSITIONS // size, one, 0)


def norm_kernel(core, own, sibling, gain):
    width = own.shape[1]
    return pl.pallas_call(
        norm_body,
        out_shape=jax.ShapeDtypeStruct((PAD + ROWS, width), bf16),
        in_specs=[pl.BlockSpec(memory_space=pltpu.SMEM)]
        + [pl.BlockSpec(memory_space=pltpu.VMEM) for _ in range(3)],
        compiler_params=params(),
        name="norm",
    )(core, own, sibling, gain)


def tail_body(rows, gain, normed, out):
    out[...] = norm_rows(rows[...], gain[...])


def tail_kernel(rows, gain, normed):
    return pl.pallas_call(
        tail_body,
        out_shape=jax.ShapeDtypeStruct(normed.shape, bf16),
        grid=(1,),
        in_specs=[whole(rows.shape), whole(gain.shape), pl.BlockSpec(memory_space=pl.ANY)],
        out_specs=pl.BlockSpec(rows.shape, lambda i: (0, 0)),
        input_output_aliases={2: 0},
        compiler_params=params(),
        name="tail",
    )(rows, gain, normed)


def decay_body(core, own, other, cum_r, columns, fades):
    count = OWN // HEADDIM
    heads = COLS // HEADDIM
    mine = own[pl.ds(pl.multiple_of(core[0] * count, count), count), :]
    earlier = jnp.where(core[0] == 0, mine, other[...])
    later = jnp.where(core[0] == 0, other[...], mine)
    per = POSITIONS // GROUP
    rows = jnp.concatenate(
        [a[:, GROUP * j : GROUP * j + GROUP] for a in (earlier, later) for j in range(per)], axis=0
    )
    row = lax.broadcasted_iota(jnp.int32, (GROUP, GROUP), 0)
    lane = lax.broadcasted_iota(jnp.int32, (GROUP, GROUP), 1)
    upto = jnp.where(row <= lane, 1.0, 0.0).astype(f32)
    cum = jnp.dot(rows, upto, preferred_element_type=f32, precision=lax.Precision.HIGHEST)
    before = [jnp.zeros((count, 1), f32)]
    for j in range(BLOCKS):
        before.append(before[-1] + cum[count * j : count * j + count, GROUP - 1 : GROUP])
    since = cum + jnp.concatenate(before[:BLOCKS], axis=0)
    step = -rows
    log_step = jnp.where(step > 0.0, jnp.log(jnp.where(step > 0.0, step, 1.0)), -1e30)
    two_r = (cum - log_step) * LOG2E
    turned = [a.T for a in (cum * LOG2E, two_r, since * LOG2E)]
    fill = jnp.zeros((GROUP, 128 - 3 * count), f32)
    for j in range(BLOCKS):
        some = slice(count * j, count * j + count)
        columns[GROUP * j : GROUP * j + GROUP, :] = jnp.concatenate(
            [a[:, some] for a in turned] + [fill], axis=1
        )
    for i in range(OWN // COLS):
        for j in range(BLOCKS):
            at = slice(GROUP * j, GROUP * j + GROUP)
            some = slice(count * j + heads * i, count * j + heads * i + heads)
            cum_r[i, :, at] = two_r[some, :]
    fade = jnp.broadcast_to(jnp.exp(before[BLOCKS]), (count, 128))
    first = lax.broadcasted_iota(jnp.int32, (1, 128), 1) < HEADDIM
    pairs = OWN // 128
    spread_out = jnp.concatenate(
        [jnp.where(first, fade[2 * p : 2 * p + 1], fade[2 * p + 1 : 2 * p + 2]) for p in range(pairs)],
        axis=0,
    )
    high = spread_out.astype(bf16).astype(f32)
    fades[...] = jnp.concatenate([high, spread_out - high], axis=0).astype(bf16)


def decay_kernel(core, own, other):
    steps = OWN // COLS
    heads = COLS // HEADDIM
    return pl.pallas_call(
        decay_body,
        out_shape=(
            jax.ShapeDtypeStruct((steps, heads, ROWS), f32),
            jax.ShapeDtypeStruct((ROWS, 128), f32),
            jax.ShapeDtypeStruct((PAD, 128), bf16),
        ),
        in_specs=[pl.BlockSpec(memory_space=pltpu.SMEM)]
        + [pl.BlockSpec(memory_space=pltpu.VMEM) for _ in range(2)],
        compiler_params=params(),
        name="decay",
    )(core, own, other)


def on_device(
    tokens, in_gain, in_weight, conv_weight, conv_bias, log_decay, skip, out_gain, scan_order
):
    seq = lax.axis_index("seq")
    core = seq % 2
    y = seq // 2
    swap = [(i, i ^ 1) for i in range(2 * Y)]
    onward = [(i, i + 2) for i in range(2 * Y - 2)]
    head_count = OWN // HEADDIM
    which = core.astype(jnp.int32)[None]

    first_half = sum(PARTS[:1]) * COLS

    def weight_columns(start, count):
        return lax.dynamic_slice_in_dim(in_weight, start, count, 1)

    weight = jnp.concatenate(
        [
            weight_columns(core * OWN, first_half),
            weight_columns(2 * OWN + core * STATE, STATE),
            weight_columns(core * OWN + first_half, OWN - first_half),
        ],
        axis=1,
    )
    half = lax.dynamic_slice_in_dim(weight, (y % 2) * 32, 32, 0)
    far = spread(copies(half, far_groups()), far_groups()).reshape(128, STATE + OWN)
    starts = [sum(PARTS[:g]) for g in range(len(PARTS) + 1)]
    cuts = [0] + [STATE + COLS * start for start in starts[1:]]
    far_chunks = [copies(far[:, a:b], near_groups()) for a, b in zip(cuts, cuts[1:])]
    chunks = [spread(far_chunks[0], near_groups())]

    own = tokens[0]
    gain = in_gain[None, :]
    sibling = lax.ppermute(own, "seq", swap)
    tail = jnp.where(core == 1, own[POSITIONS - PAD :], sibling[POSITIONS - PAD :])
    tail = lax.ppermute(tail, "seq", onward)
    normed = norm_kernel(which, own, sibling, gain)
    other = lax.dynamic_slice_in_dim(log_decay[0], (1 - core) * head_count, head_count, 0)
    decays = decay_kernel(which, log_decay[0], lax.ppermute(other, "seq", swap))
    bias = conv_bias[None, :]
    last_gain = out_gain[None, :]
    order = scan_order[:, None]

    normed, tail, decays, bias, last_gain, order, far_chunks = lax.optimization_barrier(
        (normed, tail, decays, bias, last_gain, order, far_chunks)
    )
    cum_r, columns, fades = decays
    normed = tail_kernel(tail, gain, normed)
    chunks.append(spread(far_chunks[1], near_groups()))

    mine = bc_kernel(which, normed, chunks[0], conv_weight, bias)
    theirs = lax.ppermute(mine, "seq", swap)
    same_core = [list(range(c, 2 * Y, 2)) for c in range(2)]
    earlier = ()
    for g, steps in enumerate(PARTS):
        earlier = heads_kernel(
            which, starts[g], steps, normed, chunks[g], conv_weight, bias, mine, theirs, columns, cum_r,
            skip, fades, earlier,
        )
        if g + 2 < len(PARTS):
            following, sent = lax.optimization_barrier((far_chunks[g + 2], earlier[1]))
            earlier = (earlier[0], sent)
            chunks.append(spread(following, near_groups()))
    local, sent = earlier
    parts = lax.all_to_all(sent, "seq", 0, 0, axis_index_groups=same_core, tiled=True)
    entering = lax.all_to_all(
        chain_kernel(parts), "seq", 0, 0, axis_index_groups=same_core, tiled=True
    )
    outgoing = finish_kernel(which, local, mine, theirs, entering, columns, last_gain, order)
    back = lax.all_to_all(outgoing, "seq", 0, 0, tiled=True)
    return regroup_kernel(back.reshape(Y, 2, 2, POSITIONS // (2 * Y), OWN))[None]


def solution(mesh):
    in_specs = (
        P("dp", "seq", None),
        P(),
        P("dp", None),
        P(),
        P(),
        P("dp", None, "seq"),
        P(),
        P(),
        P(),
    )
    out_specs = P("dp", "seq", None)
    return jax.shard_map(
        on_device, mesh=mesh, in_specs=in_specs, out_specs=out_specs, check_vma=False
    )
```

```python
import functools

import jax
import jax.numpy as jnp
from jax import lax
from jax.experimental import pallas as pl
from jax.experimental.pallas import tpu as pltpu
from jax.sharding import PartitionSpec as P

HEADDIM = 64
STATE = 128
GROUP = 128
POSITIONS = 512
ROWS = 1024
PAD = 16
BLOCKS = ROWS // GROUP
OWN = 1024
COLS = 256
PARTS = (2, 2)
LOG2E = 1.4426950408889634
EPS = 1e-05

Z, X, Y = 8, 4, 8
bf16 = jnp.bfloat16
f32 = jnp.float32


def place(z, x, y, core):
    return (z * X + x) * (2 * Y) + 2 * y + core


def far_groups():
    return [
        [place(2 * k + dz, x, y, c) for k in range(Z // 2)]
        for dz in range(2)
        for x in range(X)
        for y in range(Y)
        for c in range(2)
    ]


def near_groups():
    return [
        [place(2 * zp + dz, x, 2 * yp + dy, c) for dz in range(2) for x in range(X) for dy in range(2)]
        for zp in range(Z // 2)
        for yp in range(Y // 2)
        for c in range(2)
    ]


def copies(block, groups):
    return jnp.broadcast_to(block[None], (len(groups[0]),) + block.shape)


def spread(sent, groups):
    return lax.all_to_all(sent, ("dp", "seq"), 0, 0, axis_index_groups=groups, tiled=True)


def params():
    return pltpu.CompilerParams(vmem_limit_bytes=58 * 1024 * 1024)


def whole(shape):
    return pl.BlockSpec(shape, lambda *_: (0,) * len(shape))


def project(normed, w, w_all, p_all):
    for k in range(4):
        w_all[512 * k : 512 * k + 512, :] = w[:, 32 * k : 32 * k + 32, :].reshape(512, w.shape[2])
    p_all[...] = (
        jnp.dot(normed[...], w_all[...], preferred_element_type=f32).astype(bf16).astype(f32)
    )


def mixed_rows(start, taps, bias, p_all):
    rows = p_all.at[pl.ds(pl.multiple_of(start + 8, 8), GROUP + 8), :]
    pre = bias[...] + taps[0:1, :] * rows[5 : 5 + GROUP, :]
    for k in range(1, 4):
        pre = pre + taps[k : k + 1, :] * rows[5 + k : 5 + k + GROUP, :]
    half = 0.5 * pre
    return (half + half * jnp.tanh(half)).astype(bf16)


def bc_body(core, normed, w, taps, bias, out, w_all, p_all):
    project(normed, w, w_all, p_all)

    def one(j, carry):
        start = pl.multiple_of(j * GROUP, GROUP)
        out[pl.ds(start, GROUP), :] = mixed_rows(start, taps, bias, p_all)
        return carry

    lax.fori_loop(0, BLOCKS, one, 0, unroll=2)


def bc_kernel(core, normed, w, taps, bias):
    last = w.shape[2] // STATE - 1

    def channels(i, core):
        return (0, 2 * OWN // STATE + core[0])

    return pl.pallas_call(
        bc_body,
        out_shape=jax.ShapeDtypeStruct((ROWS, STATE), bf16),
        grid_spec=pltpu.PrefetchScalarGridSpec(
            num_scalar_prefetch=1,
            grid=(1,),
            in_specs=[
                whole(normed.shape),
                pl.BlockSpec((16, 128, STATE), lambda i, core: (0, 0, last)),
                pl.BlockSpec((4, STATE), channels),
                pl.BlockSpec((1, STATE), channels),
            ],
            out_specs=whole((ROWS, STATE)),
            scratch_shapes=[pltpu.VMEM((2048, STATE), bf16), pltpu.VMEM((PAD + ROWS, STATE), f32)],
        ),
        compiler_params=params(),
        name="bc",
    )(core, normed, w, taps, bias)


def turned_to(columns, step):
    return pltpu.roll(columns, lax.rem(128 - step * (COLS // HEADDIM), 128), 1)


def heads_body(
    base, core, normed, w, taps, bias, mine, other, columns, cum_r, skip, fades, *refs,
):
    local, sent, w_all, p_all, state = refs[-5:]
    i = pl.program_id(0)

    @pl.when(i == 0)
    def _():
        if base:
            sent[...] = refs[1][...]
        else:
            for y in range(Y):
                sent[y, sent.shape[1] - PAD :, :] = fades[...]

    project(normed, w, w_all, p_all)
    state[...] = jnp.zeros_like(state)
    heads = COLS // HEADDIM
    pairs = COLS // 128
    head = core[0] * (OWN // HEADDIM) + (base + i) * heads
    row = lax.broadcasted_iota(jnp.int32, (GROUP, GROUP), 0)
    lane = lax.broadcasted_iota(jnp.int32, (GROUP, GROUP), 1)
    causal = lane <= row
    first = lane < HEADDIM
    of_first = jnp.where(first, 1.0, 0.0).astype(bf16)
    of_second = jnp.where(first, 0.0, 1.0).astype(bf16)

    def one(j, carry):
        start = pl.multiple_of(j * GROUP, GROUP)
        here = pl.ds(start, GROUP)
        mixed = mixed_rows(start, taps, bias, p_all)
        ours, theirs = mine[here, :], other[here, :]
        b = jnp.where(core[0] == 0, ours, theirs)
        c = jnp.where(core[0] == 0, theirs, ours)
        scores = lax.dot_general(c, b, (((1,), (1,)), ((), ())), preferred_element_type=f32)
        cols = turned_to(columns[here, :], base + i)

        def by_row(h):
            return jnp.broadcast_to(cols[:, h : h + 1], (GROUP, GROUP))

        for pair in range(pairs):
            wide = slice(128 * pair, 128 * pair + 128)
            x = mixed[:, wide].astype(f32)
            weights, cums = [], []
            for h in (2 * pair, 2 * pair + 1):
                cum = by_row(h)
                cums.append(cum)
                gap = cum - cum_r[0, h : h + 1, here]
                weights.append((scores * jnp.exp2(jnp.where(causal, gap, -1e30))).astype(bf16))
            both = jnp.concatenate(weights, axis=1)
            apart = jnp.concatenate(
                [mixed[:, wide] * of_first, mixed[:, wide] * of_second], axis=0
            )
            intra = jnp.dot(both, apart, preferred_element_type=f32)
            cum = jnp.where(first, cums[0], cums[1])
            rest = jnp.where(first, by_row(16 + 2 * pair), by_row(17 + 2 * pair))
            scaled = (jnp.exp2(cum[GROUP - 1 :, :] - rest) * x).astype(bf16)
            block_state = lax.dot_general(
                b, scaled, (((0,), (0,)), ((), ())), preferred_element_type=f32
            )
            entering = state[pair]
            fade = jnp.exp2(cum)
            inter = fade * jnp.dot(c, entering.astype(bf16), preferred_element_type=f32)
            gains = jnp.where(first, skip[head + 2 * pair], skip[head + 2 * pair + 1])
            local[here, wide] = (intra + inter + gains * x).astype(bf16)
            state[pair] = fade[GROUP - 1 :, :] * entering + block_state
        return carry

    lax.fori_loop(0, BLOCKS, one, 0, unroll=4)
    slab = STATE // Y
    for y in range(Y):
        for pair in range(pairs):
            at = pl.multiple_of(((base + i) * pairs + pair) * slab, slab)
            sent[y, pl.ds(at, slab), :] = state[pair, slab * y : slab * y + slab, :].astype(bf16)


def heads_kernel(
    core, base, steps, normed, w, taps, bias, mine, other, columns, cum_r, skip, fades, earlier,
):
    heads = COLS // HEADDIM
    sent = (Y, OWN // 128 * (STATE // Y) + PAD, 128)

    def channels(i, core):
        return (0, core[0] * (OWN // COLS) + base + i)

    def step(i, core):
        return (base + i, 0, 0)

    return pl.pallas_call(
        functools.partial(heads_body, base),
        out_shape=(
            jax.ShapeDtypeStruct((ROWS, OWN), bf16),
            jax.ShapeDtypeStruct(sent, bf16),
        ),
        grid_spec=pltpu.PrefetchScalarGridSpec(
            num_scalar_prefetch=1,
            grid=(steps,),
            in_specs=[
                whole(normed.shape),
                pl.BlockSpec((16, 128, COLS), lambda i, core: (0, 0, i)),
                pl.BlockSpec((4, COLS), channels),
                pl.BlockSpec((1, COLS), channels),
                whole(mine.shape),
                whole(other.shape),
                whole(columns.shape),
                pl.BlockSpec((1, heads, ROWS), step),
                pl.BlockSpec(memory_space=pltpu.SMEM),
                whole(fades.shape),
            ]
            + ([pl.BlockSpec(memory_space=pl.ANY), whole(sent)] if earlier else []),
            out_specs=(
                pl.BlockSpec((ROWS, COLS), lambda i, core: (0, base + i)),
                whole(sent),
            ),
            scratch_shapes=[
                pltpu.VMEM((2048, COLS), bf16),
                pltpu.VMEM((PAD + ROWS, COLS), f32),
                pltpu.VMEM((COLS // 128, STATE, 128), f32),
            ],
        ),
        input_output_aliases={11: 0, 12: 1} if earlier else {},
        compiler_params=params(),
        name="heads",
    )(
        core, normed, w, taps, bias, mine, other, columns, cum_r, skip, fades, *earlier,
    )


def chain_body(parts, out):
    slab = STATE // Y
    pairs = OWN // 128
    base = pairs * slab
    for pair in range(pairs):
        rows = slice(pair * slab, pair * slab + slab)
        entering = jnp.zeros((slab, 128), f32)
        for y in range(Y):
            out[y, rows, :] = entering.astype(bf16)
            fades = parts[y, base:, :].astype(f32)
            fade = fades[pair : pair + 1] + fades[pairs + pair : pairs + pair + 1]
            entering = fade * entering + parts[y, rows, :].astype(f32)


def chain_kernel(parts):
    return pl.pallas_call(
        chain_body,
        out_shape=jax.ShapeDtypeStruct((Y, parts.shape[1] - PAD, 128), bf16),
        compiler_params=params(),
        name="chain",
    )(parts)


def finish_body(core, local, mine, other, entering, columns, gain, order, out, pick):
    @pl.when(pl.program_id(0) == 0)
    def _():
        position = lax.broadcasted_iota(jnp.int32, (POSITIONS, POSITIONS), 1)
        pick[...] = jnp.where(position == order[...], 1.0, 0.0).astype(bf16)

    heads = COLS // HEADDIM
    row = lax.broadcasted_iota(jnp.int32, (COLS, COLS), 0)
    lane = lax.broadcasted_iota(jnp.int32, (COLS, COLS), 1)
    same_head = jnp.where(row // HEADDIM == lane // HEADDIM, 1.0 / HEADDIM, 0.0).astype(bf16)
    wanted = 2 * (OWN // HEADDIM) + pl.program_id(0) * heads
    source = lax.broadcasted_iota(jnp.int32, (GROUP, COLS), 0)
    channel = lax.broadcasted_iota(jnp.int32, (GROUP, COLS), 1)
    by_head = jnp.where(source == wanted + channel // HEADDIM, 1.0, 0.0).astype(bf16)
    kept = lax.broadcasted_iota(jnp.int32, (1, GROUP), 1) >= 2 * (OWN // HEADDIM)
    states = [
        entering[:, p * (STATE // Y) : (p + 1) * (STATE // Y), :].reshape(STATE, 128)
        for p in range(COLS // 128)
    ]
    state = jnp.concatenate(states, axis=1)

    for frame in range(ROWS // POSITIONS):
        here = slice(frame * POSITIONS, (frame + 1) * POSITIONS)
        fades = jnp.exp2(jnp.where(kept, columns[here, :], 0.0))
        high = fades.astype(bf16)
        low = (fades - high.astype(f32)).astype(bf16)
        fade = jnp.dot(high, by_head, preferred_element_type=f32) + jnp.dot(
            low, by_head, preferred_element_type=f32
        )
        c = jnp.where(core[0] == 0, other[here, :], mine[here, :])
        inter = jnp.dot(c, state, preferred_element_type=f32)
        ssm = local[here, :].astype(f32) + fade * inter
        mean = jnp.dot((ssm * ssm).astype(bf16), same_head, preferred_element_type=f32)
        normalized = (ssm * lax.rsqrt(mean + EPS) * gain[...]).astype(bf16)
        picked = jnp.dot(pick[...], normalized, preferred_element_type=f32).astype(bf16)
        out[:, frame] = picked.reshape(2 * Y, POSITIONS // (2 * Y), COLS)


def finish_kernel(core, local, mine, other, entering, columns, gain, order):
    steps = OWN // COLS
    piece = POSITIONS // (2 * Y)

    def column(i, core):
        return (0, i)

    return pl.pallas_call(
        finish_body,
        out_shape=jax.ShapeDtypeStruct((2 * Y, 2, piece, OWN), bf16),
        grid_spec=pltpu.PrefetchScalarGridSpec(
            num_scalar_prefetch=1,
            grid=(steps,),
            in_specs=[
                pl.BlockSpec((ROWS, COLS), column),
                whole(mine.shape),
                whole(other.shape),
                pl.BlockSpec((Y, COLS // 128 * (STATE // Y), 128), lambda i, core: (0, i, 0)),
                whole(columns.shape),
                pl.BlockSpec((1, COLS), lambda i, core: (0, core[0] * steps + i)),
                whole(order.shape),
            ],
            out_specs=pl.BlockSpec((2 * Y, 2, piece, COLS), lambda i, core: (0, 0, 0, i)),
            scratch_shapes=[pltpu.VMEM((POSITIONS, POSITIONS), bf16)],
        ),
        compiler_params=params(),
        name="finish",
    )(core, local, mine, other, entering, columns, gain, order)


def regroup_body(part, out, pick):
    frames = 2 * Y

    @pl.when(pl.program_id(0) == 0)
    def _():
        row = lax.broadcasted_iota(jnp.int32, pick.shape, 0)
        col = lax.broadcasted_iota(jnp.int32, pick.shape, 1)
        each = pick.shape[0] // frames
        pick[...] = jnp.where(col == (row % frames) * each + row // frames, 1.0, 0.0).astype(bf16)

    rows = part[...].reshape(pick.shape[0], OWN)
    out[...] = jnp.dot(pick[...], rows, preferred_element_type=f32).astype(bf16)


def regroup_kernel(part):
    each = POSITIONS // (2 * Y) // 2
    rows = POSITIONS // 2
    return pl.pallas_call(
        regroup_body,
        out_shape=jax.ShapeDtypeStruct((POSITIONS, 2 * OWN), bf16),
        grid=(4,),
        in_specs=[pl.BlockSpec((Y, None, 2, each, OWN), lambda i: (0, i % 2, 0, i // 2, 0))],
        out_specs=pl.BlockSpec((rows, OWN), lambda i: (i // 2, i % 2)),
        scratch_shapes=[pltpu.VMEM((rows, rows), bf16)],
        compiler_params=params(),
        name="regroup",
    )(part)


def norm_rows(rows, gain):
    widened = rows.astype(f32)
    inverse = lax.rsqrt(jnp.mean(widened * widened, axis=1, keepdims=True) + EPS)
    return (widened * inverse * gain).astype(bf16)


def norm_body(core, own, sibling, gain, out):
    size = 64

    def one(i, carry):
        at = pl.multiple_of(i * size, size)
        mine = pl.multiple_of(PAD + core[0] * POSITIONS + at, PAD)
        other = pl.multiple_of(PAD + (1 - core[0]) * POSITIONS + at, PAD)
        out[pl.ds(mine, size), :] = norm_rows(own[pl.ds(at, size), :], gain[...])
        out[pl.ds(other, size), :] = norm_rows(sibling[pl.ds(at, size), :], gain[...])
        return carry

    out[:PAD, :] = jnp.zeros((PAD, out.shape[1]), bf16)
    lax.fori_loop(0, POSITIONS // size, one, 0)


def norm_kernel(core, own, sibling, gain):
    width = own.shape[1]
    return pl.pallas_call(
        norm_body,
        out_shape=jax.ShapeDtypeStruct((PAD + ROWS, width), bf16),
        in_specs=[pl.BlockSpec(memory_space=pltpu.SMEM)]
        + [pl.BlockSpec(memory_space=pltpu.VMEM) for _ in range(3)],
        compiler_params=params(),
        name="norm",
    )(core, own, sibling, gain)


def tail_body(rows, gain, normed, out):
    out[...] = norm_rows(rows[...], gain[...])


def tail_kernel(rows, gain, normed):
    return pl.pallas_call(
        tail_body,
        out_shape=jax.ShapeDtypeStruct(normed.shape, bf16),
        grid=(1,),
        in_specs=[whole(rows.shape), whole(gain.shape), pl.BlockSpec(memory_space=pl.ANY)],
        out_specs=pl.BlockSpec(rows.shape, lambda i: (0, 0)),
        input_output_aliases={2: 0},
        compiler_params=params(),
        name="tail",
    )(rows, gain, normed)


def decay_body(core, own, other, cum_r, columns, fades):
    count = OWN // HEADDIM
    heads = COLS // HEADDIM
    mine = own[pl.ds(pl.multiple_of(core[0] * count, count), count), :]
    earlier = jnp.where(core[0] == 0, mine, other[...])
    later = jnp.where(core[0] == 0, other[...], mine)
    per = POSITIONS // GROUP
    rows = jnp.concatenate(
        [a[:, GROUP * j : GROUP * j + GROUP] for a in (earlier, later) for j in range(per)], axis=0
    )
    row = lax.broadcasted_iota(jnp.int32, (GROUP, GROUP), 0)
    lane = lax.broadcasted_iota(jnp.int32, (GROUP, GROUP), 1)
    upto = jnp.where(row <= lane, 1.0, 0.0).astype(f32)
    cum = jnp.dot(rows, upto, preferred_element_type=f32, precision=lax.Precision.HIGHEST)
    before = [jnp.zeros((count, 1), f32)]
    for j in range(BLOCKS):
        before.append(before[-1] + cum[count * j : count * j + count, GROUP - 1 : GROUP])
    since = cum + jnp.concatenate(before[:BLOCKS], axis=0)
    step = -rows
    log_step = jnp.where(step > 0.0, jnp.log(jnp.where(step > 0.0, step, 1.0)), -1e30)
    two_r = (cum - log_step) * LOG2E
    turned = [a.T for a in (cum * LOG2E, two_r, since * LOG2E)]
    fill = jnp.zeros((GROUP, 128 - 3 * count), f32)
    for j in range(BLOCKS):
        some = slice(count * j, count * j + count)
        columns[GROUP * j : GROUP * j + GROUP, :] = jnp.concatenate(
            [a[:, some] for a in turned] + [fill], axis=1
        )
    for i in range(OWN // COLS):
        for j in range(BLOCKS):
            at = slice(GROUP * j, GROUP * j + GROUP)
            some = slice(count * j + heads * i, count * j + heads * i + heads)
            cum_r[i, :, at] = two_r[some, :]
    fade = jnp.broadcast_to(jnp.exp(before[BLOCKS]), (count, 128))
    first = lax.broadcasted_iota(jnp.int32, (1, 128), 1) < HEADDIM
    pairs = OWN // 128
    spread_out = jnp.concatenate(
        [jnp.where(first, fade[2 * p : 2 * p + 1], fade[2 * p + 1 : 2 * p + 2]) for p in range(pairs)],
        axis=0,
    )
    high = spread_out.astype(bf16).astype(f32)
    fades[...] = jnp.concatenate([high, spread_out - high], axis=0).astype(bf16)


def decay_kernel(core, own, other):
    steps = OWN // COLS
    heads = COLS // HEADDIM
    return pl.pallas_call(
        decay_body,
        out_shape=(
            jax.ShapeDtypeStruct((steps, heads, ROWS), f32),
            jax.ShapeDtypeStruct((ROWS, 128), f32),
            jax.ShapeDtypeStruct((PAD, 128), bf16),
        ),
        in_specs=[pl.BlockSpec(memory_space=pltpu.SMEM)]
        + [pl.BlockSpec(memory_space=pltpu.VMEM) for _ in range(2)],
        compiler_params=params(),
        name="decay",
    )(core, own, other)


def on_device(
    tokens, in_gain, in_weight, conv_weight, conv_bias, log_decay, skip, out_gain, scan_order
):
    seq = lax.axis_index("seq")
    core = seq % 2
    y = seq // 2
    swap = [(i, i ^ 1) for i in range(2 * Y)]
    onward = [(i, i + 2) for i in range(2 * Y - 2)]
    head_count = OWN // HEADDIM
    which = core.astype(jnp.int32)[None]

    first_half = sum(PARTS[:1]) * COLS

    def weight_columns(start, count):
        return lax.dynamic_slice_in_dim(in_weight, start, count, 1)

    weight = jnp.concatenate(
        [
            weight_columns(core * OWN, first_half),
            weight_columns(2 * OWN + core * STATE, STATE),
            weight_columns(core * OWN + first_half, OWN - first_half),
        ],
        axis=1,
    )
    half = lax.dynamic_slice_in_dim(weight, (y % 2) * 32, 32, 0)
    far = spread(copies(half, far_groups()), far_groups()).reshape(128, STATE + OWN)
    starts = [sum(PARTS[:g]) for g in range(len(PARTS) + 1)]
    cuts = [0] + [STATE + COLS * start for start in starts[1:]]
    far_chunks = [copies(far[:, a:b], near_groups()) for a, b in zip(cuts, cuts[1:])]
    chunks = [spread(far_chunks[0], near_groups())]

    own = tokens[0]
    gain = in_gain[None, :]
    sibling = lax.ppermute(own, "seq", swap)
    tail = jnp.where(core == 1, own[POSITIONS - PAD :], sibling[POSITIONS - PAD :])
    tail = lax.ppermute(tail, "seq", onward)
    sibling, far_chunks = lax.optimization_barrier((sibling, far_chunks))
    normed = norm_kernel(which, own, sibling, gain)
    other = lax.dynamic_slice_in_dim(log_decay[0], (1 - core) * head_count, head_count, 0)
    decays = decay_kernel(which, log_decay[0], lax.ppermute(other, "seq", swap))
    bias = conv_bias[None, :]
    last_gain = out_gain[None, :]
    order = scan_order[:, None]

    normed, tail, decays, bias, last_gain, order, far_chunks = lax.optimization_barrier(
        (normed, tail, decays, bias, last_gain, order, far_chunks)
    )
    cum_r, columns, fades = decays
    normed = tail_kernel(tail, gain, normed)
    chunks.append(spread(far_chunks[1], near_groups()))

    mine = bc_kernel(which, normed, chunks[0], conv_weight, bias)
    theirs = lax.ppermute(mine, "seq", swap)
    same_core = [list(range(c, 2 * Y, 2)) for c in range(2)]
    earlier = ()
    for g, steps in enumerate(PARTS):
        earlier = heads_kernel(
            which, starts[g], steps, normed, chunks[g], conv_weight, bias, mine, theirs, columns, cum_r,
            skip, fades, earlier,
        )
        if g + 2 < len(PARTS):
            following, sent = lax.optimization_barrier((far_chunks[g + 2], earlier[1]))
            earlier = (earlier[0], sent)
            chunks.append(spread(following, near_groups()))
    local, sent = earlier
    parts = lax.all_to_all(sent, "seq", 0, 0, axis_index_groups=same_core, tiled=True)
    entering = lax.all_to_all(
        chain_kernel(parts), "seq", 0, 0, axis_index_groups=same_core, tiled=True
    )
    outgoing = finish_kernel(which, local, mine, theirs, entering, columns, last_gain, order)
    back = lax.all_to_all(outgoing, "seq", 0, 0, tiled=True)
    return regroup_kernel(back.reshape(Y, 2, 2, POSITIONS // (2 * Y), OWN))[None]


def solution(mesh):
    in_specs = (
        P("dp", "seq", None),
        P(),
        P("dp", None),
        P(),
        P(),
        P("dp", None, "seq"),
        P(),
        P(),
        P(),
    )
    out_specs = P("dp", "seq", None)
    return jax.shard_map(
        on_device, mesh=mesh, in_specs=in_specs, out_specs=out_specs, check_vma=False
    )
```
